128 devices in a mesh: seg: 8 (over x, core), sec: 16 (over z, y).
Axes of the slice: x: 4, y: 4, z: 4, core: 2. Of those that a mesh axis runs over, the one named last changes fastest.
Arguments:
- left_environment: bfloat16 [8, 128, 64, 1920], P('seg', 'sec'), may hold values from -0.125 to 0.125
- right_environment: bfloat16 [8, 128, 64, 1920], P('seg', 'sec'), may hold values from -0.75 to 0.75
- site_previous: bfloat16 [8, 128, 64, 256], P('seg', 'sec'), may hold values from -0.75 to 0.75
- state_start: float32 [8, 128, 64, 256], P('seg', 'sec'), may hold values from -36 to 36
- preconditioner: float32 [8, 128, 64, 256], P('seg', 'sec'), may hold values from 0.25 to 4
- channel_tensor: bfloat16 [30, 4, 30, 4], replicated, may hold values from -0.5 to 0.5
- channel_mask: int32 [30, 30], replicated, may hold values 0 or 1
- sector_shift: int32 [5, 128], replicated, may hold values from 0 to 127, as said below
- left_sizes: int32 [128], replicated, may hold values from 32 to 64, as said below
- right_sizes: int32 [128, 4], replicated, may hold values from 32 to 64, as said below
Outputs:
- bond_state: float32 [8, 128, 64, 256], P('seg', 'sec')
- energy: float32 [8], P('seg')
The draws below stay inside these ranges and needn't reach their ends.
Inputs may be any that keep to these rules, and one draw needn't show every extreme that they name: Each row is a permutation of the 128 sectors; for every group of 8 consecutive sectors and every other such group, at most 3 pairs of a class k and a sector l of the first group have sector_shift[k, l] in the second group, and some pair of groups reaches 3. `left_sizes`: some sector fills its tile and some has 32 live states. `right_sizes`: some block fills its tile and some has 32 live states.
All inputs are finite; a program needn't handle non-finite values.
Results may differ from the reference program's by a relative error of at most 0.012.
Values may be sent and summed in bfloat16 or wider, within the bound.
No kernel may reach another device: no remote copies, remote signals or barrier semaphores. Data moves between devices by JAX's collectives and lax.ppermute only.
A program may use at most 256 MiB of HBM per device.

```python
import jax
import jax.numpy as jnp
from jax import lax

W = 30
D = 4
B = 64
SEC_DEV = 8
CLASSES = 5
ITERS = 2
SECTORS = 128
SEGS = 8
N_SEC = 16


def sizes_with_ends(key, entries):
    first_key, second_key, third_key = jax.random.split(key, 3)
    values = jax.random.randint(first_key, (entries,), B // 2, B + 1)
    top_place = jax.random.randint(second_key, (), 0, entries)
    low_place = (top_place + 1 + jax.random.randint(third_key, (), 0, entries - 1)) % entries
    positions = jnp.arange(entries)
    values = jnp.where(positions == low_place, B // 2, values)
    values = jnp.where(positions == top_place, B, values)
    return values.astype(jnp.int32)


def draw_left_sizes(key, part):
    return sizes_with_ends(jax.random.fold_in(key, 11), SECTORS)


def draw_right_sizes(key, part):
    return sizes_with_ends(jax.random.fold_in(key, 23), SECTORS * D).reshape(SECTORS, D)


def draw_sector_shift(key, part):
    group_count = SECTORS // SEC_DEV
    first_key, second_key = jax.random.split(jax.random.fold_in(key, 37))
    relabel = jax.random.permutation(first_key, group_count)
    slot_keys = jax.random.split(second_key, CLASSES * group_count)
    slot_order = jax.vmap(lambda one_key: jax.random.permutation(one_key, SEC_DEV))(slot_keys)
    slot_order = slot_order.reshape(CLASSES, group_count, SEC_DEV)
    sector = jnp.arange(SECTORS, dtype=jnp.int32)
    group = sector // SEC_DEV
    local = sector % SEC_DEV
    charge = jnp.arange(CLASSES, dtype=jnp.int32)[:, None]
    raw_owner = (group[None, :] + charge * SEC_DEV + local[None, :]) % group_count
    owner = relabel[raw_owner]
    slot = slot_order[charge, owner, local[None, :]]
    return (owner * SEC_DEV + slot).astype(jnp.int32)


def sector_ramp(top):
    fraction = jnp.arange(SECTORS, dtype=jnp.float32) / float(SECTORS - 1)
    return jnp.exp(jnp.log(top) * fraction)[None, :, None, None]


def draw_state_start(key, part):
    shape = (SEGS, SECTORS, B, D * B)
    inner_key = jax.random.fold_in(key, 51)
    base = jnp.clip(jax.random.normal(inner_key, shape, jnp.float32), -6.0, 6.0)
    return base * sector_ramp(6.0)


def draw_preconditioner(key, part):
    shape = (SEGS, SECTORS, B, D * B)
    inner_key = jax.random.fold_in(key, 67)
    base = jnp.exp(jax.random.uniform(inner_key, shape, jnp.float32, jnp.log(0.25), 0.0))
    return base * sector_ramp(4.0)


def set_ends(drawn, stream_key, least, high):
    index_at = [jax.random.randint(jax.random.fold_in(stream_key, axis), (), 0, length) for axis, length in enumerate(drawn.shape)]
    main_axis = drawn.shape.index(max(drawn.shape))
    next_to = index_at[:main_axis] + [(index_at[main_axis] + 1) % drawn.shape[main_axis]] + index_at[main_axis + 1:]
    return drawn.at[tuple(index_at)].set(least).at[tuple(next_to)].set(high)


def block_scale(own_key, dims, pieces, smallest, high):
    loudness, own = 1.0, jax.random.fold_in(own_key, 6)
    for axis_at, blocks in pieces:
        draws = jnp.exp(jax.random.uniform(jax.random.fold_in(own, axis_at), (blocks,), jnp.float32, smallest / len(pieces), high / len(pieces)))
        loudness = loudness * jnp.repeat(draws, dims[axis_at] // blocks).reshape([-1 if axis == axis_at else 1 for axis in range(len(dims))])
    return loudness


def gaussian(key, shape, deviation, bound, shards=(), held_as=jnp.bfloat16):
    values = deviation * jax.random.normal(key, shape, jnp.float32)
    if shards:
        values = values * block_scale(key, shape, shards, -0.22, 0.18)
    return jnp.clip(values, -bound, bound).astype(held_as)


def setup_inputs(seed: int = 0) -> dict:
    streams_of = jax.random.split(jax.random.key(seed), 11)
    return {
        "left_environment": gaussian(streams_of[0], (SEGS, SECTORS, B, W * B), (W * B) ** -0.5, 0.125, ((0, 8), (1, 16))),
        "right_environment": gaussian(streams_of[1], (SEGS, SECTORS, B, W * B), B ** -0.5, 0.75, ((0, 8), (1, 16))),
        "site_previous": gaussian(streams_of[2], (SEGS, SECTORS, B, D * B), B ** -0.5, 0.75, ((0, 8), (1, 16))),
        "state_start": draw_state_start(jax.random.fold_in(streams_of[10], 71), 0),
        "preconditioner": draw_preconditioner(jax.random.fold_in(streams_of[10], 71), 0),
        "channel_tensor": gaussian(streams_of[5], (W, D, W, D), (W * D) ** -0.5, 0.5),
        "channel_mask": set_ends((jax.random.randint(streams_of[6], (W, W), 0, 2) < 1).astype(jnp.int32), jax.random.fold_in(streams_of[6], 1), 0, 1),
        "sector_shift": draw_sector_shift(jax.random.fold_in(streams_of[10], 71), 0),
        "left_sizes": draw_left_sizes(jax.random.fold_in(streams_of[10], 71), 0),
        "right_sizes": draw_right_sizes(jax.random.fold_in(streams_of[10], 71), 0),
    }


EPSILON = 1e-06
HIGHEST_PRECISION = lax.Precision.HIGHEST

def live_masks(left_sizes, right_sizes):
    row_live = jnp.arange(B, dtype=jnp.int32)[None, :] < left_sizes[:, None]
    column_live = jnp.arange(B, dtype=jnp.int32)[None, None, :] < right_sizes[:, :, None]
    joined_live = row_live[:, :, None, None] & column_live[:, None, :, :]
    return joined_live.astype(jnp.float32).reshape(SECTORS, B, D * B)

def build_environment(environment, site_blocks, channel_mix, sector_shift):
    groups = W // CLASSES
    split_left = environment.astype(jnp.float32).reshape(SECTORS, B, CLASSES, groups, B)
    tensor = site_blocks.astype(jnp.float32).reshape(SECTORS, B, D, B)
    contracted = jnp.einsum('lpkja,lasb->lpkjsb', split_left, tensor, precision=HIGHEST_PRECISION).astype(jnp.bfloat16)
    channel_split = channel_mix.reshape(CLASSES, groups, D, W, D)
    accumulated = jnp.zeros((SECTORS, B, W, B), jnp.float32)
    for charge in range(CLASSES):
        shifted_site = jnp.take(tensor, sector_shift[charge], axis=0)
        carried = jnp.einsum('jtvs,lpjsb->lptvb', channel_split[charge], contracted[:, :, charge].astype(jnp.float32), precision=HIGHEST_PRECISION).astype(jnp.bfloat16)
        accumulated = accumulated + jnp.einsum('lpte,lptvb->levb', shifted_site, carried.astype(jnp.float32), precision=HIGHEST_PRECISION)
    return accumulated.astype(jnp.bfloat16).reshape(SECTORS, B, W * B)

def apply_operator(vector_low, left_split, right_split, channel_mix, sector_shift, live_mask):
    blocks = vector_low.astype(jnp.float32).reshape(SECTORS, B, D, B)
    right_product = jnp.einsum('lasb,lbvc->lasvc', blocks, right_split, precision=HIGHEST_PRECISION).astype(jnp.bfloat16)
    mixed_product = jnp.einsum('wtvs,lasvc->lwatc', channel_mix, right_product.astype(jnp.float32), precision=HIGHEST_PRECISION).astype(jnp.bfloat16)
    grouped = mixed_product.astype(jnp.float32).reshape(SECTORS, CLASSES, W // CLASSES, B, D, B)
    partial_value = jnp.einsum('lpkja,lkjatc->lkptc', left_split, grouped, precision=HIGHEST_PRECISION)
    partial_value = partial_value.reshape(N_SEC, SEC_DEV, CLASSES, B * D * B)
    onehot = (sector_shift[:, :, None] == jnp.arange(SECTORS, dtype=jnp.int32)[None, None, :]).astype(jnp.float32)
    onehot = onehot.reshape(CLASSES, N_SEC, SEC_DEV, SECTORS)
    group_sums = jnp.einsum('kgim,gikx->gmx', onehot, partial_value, precision=HIGHEST_PRECISION)
    rounded = lax.optimization_barrier(group_sums.astype(jnp.bfloat16)).astype(jnp.float32)
    return live_mask * lax.optimization_barrier(jnp.sum(rounded, axis=0)).reshape(SECTORS, B, D * B)

def reference(left_environment, right_environment, site_previous, state_start, preconditioner, channel_tensor, channel_mask, sector_shift, left_sizes, right_sizes):
    channel_mix = channel_tensor.astype(jnp.float32) * channel_mask.astype(jnp.float32)[:, None, :, None]
    live_mask = live_masks(left_sizes, right_sizes)

    def solve_segment(segment):
        before = jnp.maximum(segment - 1, 0).astype(jnp.int32)
        following = jnp.minimum(segment + 1, SEGS - 1).astype(jnp.int32)
        handed = build_environment(left_environment[before], site_previous[before], channel_mix, sector_shift)
        left_used = jnp.where(segment == 0, left_environment[segment], handed)
        right_used = right_environment[following]
        left_split = left_used.astype(jnp.float32).reshape(SECTORS, B, CLASSES, W // CLASSES, B)
        right_split = right_used.astype(jnp.float32).reshape(SECTORS, B, W, B)
        entries = float(SECTORS * B * D * B)

        def inner(vector_one, vector_two):
            return jnp.sum(vector_one * vector_two) / entries

        def operator(vector):
            return apply_operator(vector.astype(jnp.bfloat16), left_split, right_split, channel_mix, sector_shift, live_mask)
        current = live_mask * state_start[segment]
        current = current / jnp.sqrt(inner(current, current) + EPSILON)
        applied = operator(current)
        precondition = preconditioner[segment]
        for iteration in range(ITERS):
            rayleigh_value = inner(current, applied)
            correction = precondition * (applied - rayleigh_value * current)
            correction = correction - inner(current, correction) * current
            direction = correction / jnp.sqrt(inner(correction, correction) + EPSILON)
            product = operator(direction)
            cross_term = 0.5 * (inner(current, product) + inner(direction, applied))
            far_term = inner(direction, product)
            rotation = 0.5 * jnp.arctan2(-2.0 * cross_term, far_term - rayleigh_value)
            current = jnp.cos(rotation) * current + jnp.sin(rotation) * direction
            applied = jnp.cos(rotation) * applied + jnp.sin(rotation) * product
        return (current, inner(current, applied))
    bond_state, energy = lax.map(solve_segment, jnp.arange(SEGS, dtype=jnp.int32))
    return (bond_state, energy)
```

```python
import functools

import jax
import jax.numpy as jnp
from jax import lax
from jax.experimental import pallas as pl
from jax.experimental.pallas import tpu as pltpu
from jax.sharding import PartitionSpec as P

W = 30
D = 4
B = 64
SEC_DEV = 8
CLASSES = 5
GROUP = W // CLASSES
PAIRS = SEC_DEV * CLASSES
HALF = B // 2
FOLD = 2 * B
ROWS = W * HALF
TILE = D * HALF
MIX = 128
EPSILON = 1e-06
BF = jnp.bfloat16
F32 = jnp.float32


def passed_along(block, axis, distance):
    devices = range(lax.axis_size(axis))
    route = [(i - distance, i) for i in devices if i - distance in devices]
    return lax.ppermute(block, axis, route)


def low_lanes(rows):
    return lax.broadcasted_iota(jnp.int32, (rows, FOLD), 1) < B


def fold_pair(pair):
    stacked = jnp.concatenate([pair, pltpu.roll(pair, FOLD - HALF, 1)], axis=0)
    turned = stacked.T
    return turned[:HALF], turned[B : B + HALF]


def unfold_pair(first, second):
    filler = jnp.zeros((HALF, FOLD), F32)
    turned = jnp.concatenate([first, filler, second, filler], axis=0).T
    upper = lax.broadcasted_iota(jnp.int32, (B, FOLD), 1) % B < HALF
    return jnp.where(upper, turned[:B], pltpu.roll(turned[B:], HALF, 1))


def spread(tile):
    rolled = pltpu.roll(tile, B, 1)
    low = low_lanes(HALF)
    zero = jnp.zeros_like(tile)
    return jnp.concatenate(
        [
            jnp.where(low, tile, zero),
            jnp.where(low, rolled, zero),
            jnp.where(low, zero, rolled),
            jnp.where(low, zero, tile),
        ],
        axis=0,
    )


def spread_pair(pair):
    rolled = pltpu.roll(pair, B, 1)
    low = low_lanes(B)
    zero = jnp.zeros_like(pair)
    first = jnp.concatenate([jnp.where(low, pair, zero), jnp.where(low, zero, rolled)], axis=0)
    second = jnp.concatenate([jnp.where(low, rolled, zero), jnp.where(low, zero, pair)], axis=0)
    return first, second


def dot(left, right):
    return jnp.dot(left, right, preferred_element_type=F32)


def route_kernel(me_ref, shift_ref, site_ref, slot_ref, local_ref, take_ref, send_ref, count, source):
    groups = send_ref.shape[0]
    slots = send_ref.shape[1]
    me = me_ref[0]
    for g in range(groups):
        count[g] = 0
    for i in range(groups * slots):
        source[i] = 0
    for l in range(SEC_DEV):
        for k in range(CLASSES):
            target = shift_ref[k, me * SEC_DEV + l]
            owner = target // SEC_DEV
            rank = count[owner]
            count[owner] = rank + 1
            slot = owner * slots + jnp.minimum(rank, slots - 1)
            slot_ref[l * CLASSES + k] = jnp.where(owner == me, -1, slot)
            local_ref[l * CLASSES + k] = target % SEC_DEV

    def one_group(g, carry):
        rank = jnp.int32(0)
        for l in range(SEC_DEV):
            for k in range(CLASSES):
                target = shift_ref[k, g * SEC_DEV + l]
                hit = target // SEC_DEV == me
                place = jnp.minimum(rank, slots - 1)

                @pl.when(hit)
                def _():
                    local = target % SEC_DEV
                    take_ref[k * SEC_DEV + local] = jnp.where(g == me, -1, g * slots + place)
                    source[g * slots + place] = local

                rank = rank + hit.astype(jnp.int32)
        return carry

    lax.fori_loop(0, groups, one_group, 0)

    def one_copy(g, carry):
        for r in range(slots):
            send_ref[g, r] = site_ref[source[g * slots + r]]
        return carry

    lax.fori_loop(0, groups, one_copy, 0)


def route(me, sector_shift, site, groups, slots):
    smem = pl.BlockSpec(memory_space=pltpu.SMEM)
    vmem = pl.BlockSpec(memory_space=pltpu.VMEM)
    return pl.pallas_call(
        route_kernel,
        out_shape=(
            jax.ShapeDtypeStruct((PAIRS,), jnp.int32),
            jax.ShapeDtypeStruct((PAIRS,), jnp.int32),
            jax.ShapeDtypeStruct((PAIRS,), jnp.int32),
            jax.ShapeDtypeStruct((groups, slots, B, D * B), BF),
        ),
        in_specs=[smem, smem, vmem],
        out_specs=(smem, smem, smem, vmem),
        scratch_shapes=[pltpu.SMEM((groups,), jnp.int32), pltpu.SMEM((groups * slots,), jnp.int32)],
        name="route",
    )(me, sector_shift, site)


def fold_environment_kernel(in_ref, out_ref):
    for i in range(W // 2):
        pair = in_ref[0, :, i * FOLD : (i + 1) * FOLD].astype(F32)
        first, second = fold_pair(pair)
        out_ref[0, (2 * i) * HALF : (2 * i + 1) * HALF, :] = first.astype(BF)
        out_ref[0, (2 * i + 1) * HALF : (2 * i + 2) * HALF, :] = second.astype(BF)


def fold_environment(environment):
    return pl.pallas_call(
        fold_environment_kernel,
        grid=(SEC_DEV,),
        out_shape=jax.ShapeDtypeStruct((SEC_DEV, ROWS, FOLD), BF),
        in_specs=[pl.BlockSpec((1, B, W * B), lambda l: (l, 0, 0))],
        out_specs=pl.BlockSpec((1, ROWS, FOLD), lambda l: (l, 0, 0)),
        name="fold_environment",
        cost_estimate=pl.CostEstimate(flops=0, bytes_accessed=4 * SEC_DEV * ROWS * FOLD, transcendentals=0),
    )(environment)


def live_mask(left_size, right_sizes):
    half_p = lax.broadcasted_iota(jnp.int32, (HALF, FOLD), 1)
    column = lax.broadcasted_iota(jnp.int32, (HALF, FOLD), 0) + jnp.where(half_p < B, 0, HALF)
    row = jnp.where(half_p < B, half_p, half_p - B)
    parts = [
        jnp.where((row < left_size) & (column < right_sizes[t]), 1.0, 0.0).astype(F32) for t in range(D)
    ]
    return jnp.concatenate(parts, axis=0)


def fold_state_kernel(left_ref, right_ref, state_ref, weight_ref, start_ref, fold_ref):
    l = pl.program_id(0)
    mask = live_mask(left_ref[l], [right_ref[l * D + t] for t in range(D)])
    for source, result in ((state_ref, start_ref), (weight_ref, fold_ref)):
        tiles = []
        for i in range(D // 2):
            tiles.extend(fold_pair(source[0, :, i * FOLD : (i + 1) * FOLD]))
        folded = jnp.concatenate(tiles, axis=0)
        result[0] = mask * folded if result is start_ref else folded


def fold_state(left_sizes, right_sizes, state, weight):
    natural = pl.BlockSpec((1, B, D * B), lambda l, *refs: (l, 0, 0))
    folded = pl.BlockSpec((1, TILE, FOLD), lambda l, *refs: (l, 0, 0))
    shape = jax.ShapeDtypeStruct((SEC_DEV, TILE, FOLD), F32)
    return pl.pallas_call(
        fold_state_kernel,
        out_shape=(shape, shape),
        grid_spec=pltpu.PrefetchScalarGridSpec(
            num_scalar_prefetch=2,
            grid=(SEC_DEV,),
            in_specs=[natural, natural],
            out_specs=(folded, folded),
        ),
        name="fold_state",
        cost_estimate=pl.CostEstimate(flops=0, bytes_accessed=16 * SEC_DEV * TILE * FOLD, transcendentals=0),
    )(left_sizes, right_sizes, state, weight)


def mix_channels(mix, first, second):
    for j in range(0, HALF, 2):
        parts = [first[pl.ds(j + i, MIX, stride=HALF), :].astype(BF) for i in range(2)]
        mixed = dot(mix, jnp.concatenate(parts, axis=1))
        for i in range(2):
            second[pl.ds(j + i, MIX, stride=HALF), :] = mixed[:, i * FOLD : (i + 1) * FOLD]


def build_kernel(slot_ref, local_ref, env_ref, own_ref, came_ref, mix_ref, out_ref, first, second):
    l = pl.program_id(0)

    @pl.when(l == 0)
    def _():
        first[W * D * HALF :, :] = jnp.zeros((MIX * HALF - W * D * HALF, FOLD), F32)

    mix_turned = mix_ref[...].astype(F32).T.astype(BF)
    for k in range(CLASSES):
        slot = slot_ref[l * CLASSES + k]
        local = local_ref[l * CLASSES + k]
        tensor = jnp.where(slot < 0, own_ref[local], came_ref[jnp.maximum(slot, 0)])
        blocks = []
        for i in range(D // 2):
            blocks.extend(spread_pair(tensor[:, i * FOLD : (i + 1) * FOLD].astype(F32)))
        right = jnp.concatenate(blocks, axis=1).astype(BF)
        left = env_ref[0, k * GROUP * HALF : (k + 1) * GROUP * HALF, :]
        joined = dot(left, right)
        for j in range(GROUP):
            for t in range(D):
                at = ((k * GROUP + j) * D + t) * HALF
                first[at : at + HALF, :] = joined[j * HALF : (j + 1) * HALF, t * FOLD : (t + 1) * FOLD]
    mix_channels(mix_turned, first, second)
    own = own_ref[l]
    tiles = []
    low_half = low_lanes(HALF)
    for i in range(D // 2):
        pair = own[:, i * FOLD : (i + 1) * FOLD].astype(F32)
        rolled = pltpu.roll(pair, B, 1)
        tiles.append(jnp.where(low_half, pair[:HALF], rolled[HALF:]))
        tiles.append(jnp.where(low_half, rolled[:HALF], pair[HALF:]))
    turned = jnp.concatenate(tiles, axis=0).T.astype(BF)
    low = low_lanes(B)
    for v in range(0, W, 2):
        right = jnp.concatenate(
            [second[(v + i) * TILE : (v + i + 1) * TILE, :].astype(BF) for i in range(2)], axis=1
        )
        product = dot(turned, right)
        for i in range(2):
            block = product[:, i * FOLD : (i + 1) * FOLD]
            chosen = jnp.where(low, block[:B], block[B:])
            total = chosen + pltpu.roll(chosen, B, 1)
            folded = jnp.where(low_half, total[:HALF], total[HALF:])
            out_ref[0, (v + i) * HALF : (v + i + 1) * HALF, :] = folded.astype(BF)


def build_environment(slot, local, environment, site, came, mix):
    folded = pl.BlockSpec((1, ROWS, FOLD), lambda l, *refs: (l, 0, 0))
    whole = lambda shape: pl.BlockSpec(shape, lambda l, *refs: (0,) * len(shape))
    return pl.pallas_call(
        build_kernel,
        out_shape=jax.ShapeDtypeStruct((SEC_DEV, ROWS, FOLD), BF),
        grid_spec=pltpu.PrefetchScalarGridSpec(
            num_scalar_prefetch=2,
            grid=(SEC_DEV,),
            in_specs=[folded, whole(site.shape), whole(came.shape), whole(mix.shape)],
            out_specs=folded,
            scratch_shapes=[pltpu.VMEM((MIX * HALF, FOLD), F32), pltpu.VMEM((MIX * HALF, FOLD), F32)],
        ),
        name="build_environment",
        cost_estimate=pl.CostEstimate(flops=10**10, bytes_accessed=10**7, transcendentals=0),
    )(slot, local, environment, site, came, mix)


def gram_sums(gram_ref, entries):
    total = gram_ref[0]
    for g in range(1, gram_ref.shape[0]):
        total = total + gram_ref[g]
    row = total[:1] * (1.0 / entries)
    lane = lax.broadcasted_iota(jnp.int32, (1, FOLD), 1)
    return lambda i: jnp.sum(jnp.where(lane == i, row, 0.0), axis=1, keepdims=True)


def rotation(cross_sum, far, rayleigh_value):
    up, along = -cross_sum, far - rayleigh_value
    scale = jnp.maximum(jnp.abs(up), jnp.abs(along))
    flat = scale == 0.0
    scale = jnp.where(flat, 1.0, scale)
    up, along = up / scale, along / scale
    length = jnp.sqrt(up * up + along * along)
    length = jnp.where(flat, 1.0, length)
    larger = jnp.sqrt(0.5 * (1.0 + jnp.abs(along) / length))
    smaller = jnp.abs(up) / (2.0 * length * larger)
    ahead = along >= 0.0
    cosine = jnp.where(flat, 1.0, jnp.where(ahead, larger, smaller))
    size = jnp.where(ahead, smaller, larger)
    sine = jnp.where(flat, 0.0, jnp.where(cross_sum < 0.0, size, -size))
    return cosine, sine


def correction_scalars(xx, xa, xpa, xpx, papa, papx, pxpx):
    along = xpa - xa * xpx
    square = papa - 2.0 * xa * papx + xa * xa * pxpx
    square = square - 2.0 * along * along + along * along * xx
    return xa, along, lax.rsqrt(jnp.maximum(square, 0.0) + EPSILON)


FIRST = ("uu", "uh", "uPh", "uPu", "PhPh", "PhPu", "PuPu")
LATER = (
    "xx", "xd", "dd", "xa", "xp", "da", "dp", "xPa", "xPp", "dPa", "dPp", "xPx", "xPd", "dPd",
    "PaPa", "PaPp", "PpPp", "PaPx", "PaPd", "PpPx", "PpPd", "PxPx", "PxPd", "PdPd",
)
LAST = ("xa", "xp", "da", "dp")


def split_name(name):
    parts, at = [], 0
    while at < len(name):
        size = 2 if name[at] == "P" else 1
        parts.append(name[at : at + size])
        at += size
    return parts


def first_scalars(gram_ref, entries):
    sums = gram_sums(gram_ref, entries)
    value = {name: sums(i) for i, name in enumerate(FIRST)}
    inverse = lax.rsqrt(value["uu"] + EPSILON)
    square = inverse * inverse
    named = [value[name] * square for name in FIRST]
    return (inverse,) + correction_scalars(*named)


def later_scalars(gram_ref, entries):
    sums = gram_sums(gram_ref, entries)
    value = {name: sums(i) for i, name in enumerate(LATER)}
    cosine, sine = rotation(value["xp"] + value["da"], value["dp"], value["xa"])
    cc, cs, ss = cosine * cosine, cosine * sine, sine * sine

    def turned(a, b, c, d):
        return cc * value[a] + cs * (value[b] + value[c]) + ss * value[d]

    named = (
        turned("xx", "xd", "xd", "dd"),
        turned("xa", "xp", "da", "dp"),
        turned("xPa", "xPp", "dPa", "dPp"),
        turned("xPx", "xPd", "xPd", "dPd"),
        turned("PaPa", "PaPp", "PaPp", "PpPp"),
        turned("PaPx", "PaPd", "PpPx", "PpPd"),
        turned("PxPx", "PxPd", "PxPd", "PdPd"),
    )
    return (cosine, sine) + correction_scalars(*named)


def apply_kernel(mode, entries, *refs):
    slot_ref, local_ref, mix_ref, right_ref, left_ref = refs[:5]
    refs = refs[5:]
    l = pl.program_id(0)
    if mode == "start":
        state_ref, send_ref, own_ref, first, second, fixed = refs
    elif mode == "first":
        gram_ref, u_ref, h_ref, weight_ref = refs[:4]
        x_out, a_out, d_out, send_ref, own_ref, first, second, fixed = refs[4:]
    else:
        gram_ref, x_ref, a_ref, d_ref, p_ref, weight_ref = refs[:6]
        x_out, a_out, d_out, send_ref, own_ref, first, second, fixed = refs[6:]

    @pl.when(l == 0)
    def _():
        own_ref[...] = jnp.zeros_like(own_ref)
        first[W * D * HALF :, :] = jnp.zeros((MIX * HALF - W * D * HALF, FOLD), F32)
        if mode != "start":
            scalars = first_scalars if mode == "first" else later_scalars
            for i, value in enumerate(scalars(gram_ref, entries)):
                fixed[i : i + 1, :] = jnp.broadcast_to(value, (1, FOLD))

    if mode == "start":
        vector = state_ref[0]
    else:
        if mode == "first":
            inverse, rho, along, norm = [fixed[i : i + 1, :] for i in range(4)]
            current = inverse * u_ref[0]
            applied = inverse * h_ref[0]
        else:
            cosine, sine, rho, along, norm = [fixed[i : i + 1, :] for i in range(5)]
            current = cosine * x_ref[0] + sine * d_ref[0]
            applied = cosine * a_ref[0] + sine * p_ref[0]
        vector = (weight_ref[0] * (applied - rho * current) - along * current) * norm
        x_out[0] = current
        a_out[0] = applied
        d_out[0] = vector

    right = jnp.concatenate(
        [spread(vector[s * HALF : (s + 1) * HALF]) for s in range(D)], axis=1
    ).astype(BF)
    step = GROUP * HALF
    for i in range(CLASSES):
        product = dot(right_ref[0, i * step : (i + 1) * step, :], right)
        for v in range(GROUP):
            for s in range(D):
                at = ((i * GROUP + v) * D + s) * HALF
                first[at : at + HALF, :] = product[v * HALF : (v + 1) * HALF, s * FOLD : (s + 1) * FOLD]
    mix_channels(mix_ref[...], first, second)
    for k in range(CLASSES):
        rows, blocks = [], []
        for w in range(k * GROUP, (k + 1) * GROUP):
            rows.append(second[w * TILE : (w + 1) * TILE, :].astype(BF))
            blocks.append(spread(left_ref[0, w * HALF : (w + 1) * HALF, :].astype(F32)).astype(BF))
        partial = dot(jnp.concatenate(rows, axis=1), jnp.concatenate(blocks, axis=0))
        slot = slot_ref[l * CLASSES + k]
        local = local_ref[l * CLASSES + k]

        @pl.when(slot >= 0)
        def _():
            send_ref[jnp.maximum(slot, 0)] = partial.astype(BF)

        @pl.when(slot < 0)
        def _():
            own_ref[local] = own_ref[local] + partial


def apply_operator(mode, entries, slots_total, slot, local, mix, right_env, left_env, gram, vectors):
    vector = pl.BlockSpec((1, TILE, FOLD), lambda l, *refs: (l, 0, 0))
    folded = pl.BlockSpec((1, ROWS, FOLD), lambda l, *refs: (l, 0, 0))
    whole = lambda shape: pl.BlockSpec(shape, lambda l, *refs: (0,) * len(shape))
    shape = jax.ShapeDtypeStruct((SEC_DEV, TILE, FOLD), F32)
    kept = 0 if mode == "start" else 3
    send = jax.ShapeDtypeStruct((slots_total, TILE, FOLD), BF)
    inputs = (mix, right_env, left_env) + (() if gram is None else (gram,)) + tuple(vectors)
    return pl.pallas_call(
        functools.partial(apply_kernel, mode, entries),
        out_shape=(shape,) * kept + (send, shape),
        grid_spec=pltpu.PrefetchScalarGridSpec(
            num_scalar_prefetch=2,
            grid=(SEC_DEV,),
            in_specs=[whole(mix.shape), folded, folded]
            + ([] if gram is None else [whole(gram.shape)])
            + [vector] * len(vectors),
            out_specs=(vector,) * kept + (whole(send.shape), whole(shape.shape)),
            scratch_shapes=[
                pltpu.VMEM((MIX * HALF, FOLD), F32),
                pltpu.VMEM((MIX * HALF, FOLD), F32),
                pltpu.VMEM((8, FOLD), F32),
            ],
        ),
        name="apply_" + mode,
        cost_estimate=pl.CostEstimate(flops=10**10, bytes_accessed=10**7, transcendentals=0),
    )(slot, local, *inputs)


def collect_kernel(names, *refs):
    take_ref, left_ref, right_ref = refs[:3]
    came_ref, own_ref = refs[3:5]
    symbols = sorted({part[-1] for name in names for part in split_name(name)} - {"h", "p"})
    weighted = any("P" in name for name in names)
    vectors = refs[5 : 5 + len(symbols)]
    at = 5 + len(symbols)
    weight_ref = None
    if weighted:
        weight_ref = refs[at]
        at += 1
    out_ref, gram_ref, sums = refs[at:]
    result = "h" if names is FIRST else "p"
    m = pl.program_id(0)

    @pl.when(m == 0)
    def _():
        sums[...] = jnp.zeros_like(sums)

    total = own_ref[0]
    for k in range(CLASSES):
        place = take_ref[k * SEC_DEV + m]
        part = came_ref[jnp.maximum(place, 0)].astype(F32)
        total = total + jnp.where(place >= 0, part, 0.0)
    total = live_mask(left_ref[m], [right_ref[m * D + t] for t in range(D)]) * total
    out_ref[0] = total
    size = 8
    totals = [jnp.zeros((size, FOLD), F32) for name in names]
    for i in range(TILE // size):
        rows = slice(i * size, (i + 1) * size)
        value = {symbol: ref[0, rows, :] for symbol, ref in zip(symbols, vectors)}
        value[result] = total[rows]
        if weighted:
            weight = weight_ref[0, rows, :]
            for symbol in list(value):
                value["P" + symbol] = weight * value[symbol]
        for n, name in enumerate(names):
            one, two = split_name(name)
            totals[n] = totals[n] + value[one] * value[two]
    for n in range(len(names)):
        sums[n] = sums[n] + totals[n]

    @pl.when(m == SEC_DEV - 1)
    def _():
        lane = lax.broadcasted_iota(jnp.int32, (8, FOLD), 1)
        packed = jnp.zeros((8, FOLD), F32)
        for n in range(len(names)):
            packed = jnp.where(lane == n, jnp.sum(sums[n], keepdims=True), packed)
        for g in range(gram_ref.shape[0]):
            gram_ref[g] = packed


def collect(names, groups, take, left_sizes, right_sizes, came, own, vectors, weight):
    vector = pl.BlockSpec((1, TILE, FOLD), lambda m, *refs: (m, 0, 0))
    whole = lambda shape: pl.BlockSpec(shape, lambda m, *refs: (0,) * len(shape))
    extra = () if weight is None else (weight,)
    gram = jax.ShapeDtypeStruct((groups, 8, FOLD), F32)
    return pl.pallas_call(
        functools.partial(collect_kernel, names),
        out_shape=(jax.ShapeDtypeStruct((SEC_DEV, TILE, FOLD), F32), gram),
        grid_spec=pltpu.PrefetchScalarGridSpec(
            num_scalar_prefetch=3,
            grid=(SEC_DEV,),
            in_specs=[whole(came.shape)] + [vector] * (1 + len(vectors) + len(extra)),
            out_specs=(vector, whole(gram.shape)),
            scratch_shapes=[pltpu.VMEM((len(names), 8, FOLD), F32)],
        ),
        name="collect",
        cost_estimate=pl.CostEstimate(flops=10**7, bytes_accessed=4 * 10**6, transcendentals=0),
    )(take, left_sizes, right_sizes, came, own, *vectors, *extra)


def finish_kernel(entries, gram_ref, x_ref, d_ref, state_ref, energy_ref, fixed):
    l = pl.program_id(0)

    @pl.when(l == 0)
    def _():
        sums = gram_sums(gram_ref, entries)
        xa, xp, da, dp = [sums(i) for i in range(4)]
        cosine, sine = rotation(xp + da, dp, xa)
        energy = cosine * cosine * xa + cosine * sine * (xp + da) + sine * sine * dp
        fixed[0:1, :] = jnp.broadcast_to(cosine, (1, FOLD))
        fixed[1:2, :] = jnp.broadcast_to(sine, (1, FOLD))
        energy_ref[...] = jnp.broadcast_to(energy, energy_ref.shape)

    final = fixed[0:1, :] * x_ref[0] + fixed[1:2, :] * d_ref[0]
    for i in range(D // 2):
        first = final[(2 * i) * HALF : (2 * i + 1) * HALF]
        second = final[(2 * i + 1) * HALF : (2 * i + 2) * HALF]
        state_ref[0, :, i * FOLD : (i + 1) * FOLD] = unfold_pair(first, second)


def finish(entries, gram, current, direction):
    vector = pl.BlockSpec((1, TILE, FOLD), lambda l: (l, 0, 0))
    return pl.pallas_call(
        functools.partial(finish_kernel, entries),
        grid=(SEC_DEV,),
        out_shape=(
            jax.ShapeDtypeStruct((SEC_DEV, B, D * B), F32),
            jax.ShapeDtypeStruct((8, FOLD), F32),
        ),
        in_specs=[pl.BlockSpec(gram.shape, lambda l: (0, 0, 0)), vector, vector],
        out_specs=(
            pl.BlockSpec((1, B, D * B), lambda l: (l, 0, 0)),
            pl.BlockSpec((8, FOLD), lambda l: (0, 0)),
        ),
        scratch_shapes=[pltpu.VMEM((8, FOLD), F32)],
        name="finish",
        cost_estimate=pl.CostEstimate(flops=10**6, bytes_accessed=2 * 10**6, transcendentals=0),
    )(gram, current, direction)


def exchange(blocks):
    return lax.all_to_all(blocks, "sec", 0, 0, tiled=True)


def on_device(
    left_environment,
    right_environment,
    site_previous,
    state_start,
    preconditioner,
    channel_tensor,
    channel_mask,
    sector_shift,
    left_sizes,
    right_sizes,
):
    groups = lax.axis_size("sec")
    my_group = lax.axis_index("sec")
    offset = my_group * SEC_DEV
    slots = (PAIRS + groups - 1) // groups
    entries = float(SEC_DEV * B * D * B * groups)
    my_left = lax.dynamic_slice_in_dim(left_sizes, offset, SEC_DEV, 0)
    my_right = lax.dynamic_slice_in_dim(right_sizes, offset, SEC_DEV, 0).reshape(SEC_DEV * D)
    position = lax.axis_index("seg")
    last = lax.axis_size("seg") - 1

    came_right = passed_along(right_environment[0], "seg", -1)
    right_used = jnp.where(position == last, right_environment[0], came_right)

    slot, local, take, site_send = route(my_group[None], sector_shift, site_previous[0], groups, slots)
    site_came = exchange(site_send).reshape(groups * slots, B, D * B)
    mix = channel_tensor * channel_mask.astype(BF)[:, None, :, None]
    mix = jnp.pad(mix.reshape(W * D, W * D), ((0, MIX - W * D), (0, MIX - W * D)))

    own_left = fold_environment(left_environment[0])
    fresh = build_environment(slot, local, own_left, site_previous[0], site_came, mix)
    handed = passed_along(fresh, "seg", 1)
    left_env = jnp.where(position == 0, own_left, handed)
    right_env = fold_environment(right_used)
    start, weight = fold_state(my_left, my_right, state_start[0], preconditioner[0])

    apply = functools.partial(
        apply_operator, entries=entries, slots_total=groups * slots, slot=slot, local=local, mix=mix,
        right_env=right_env, left_env=left_env,
    )

    def gather(names, send, own, vectors, weight):
        came = exchange(send.reshape(groups, slots, TILE, FOLD)).reshape(groups * slots, TILE, FOLD)
        result, gram = collect(names, groups, take, my_left, my_right, came, own, vectors, weight)
        return result, exchange(gram)

    send, own = apply("start", gram=None, vectors=(start,))
    product, gram = gather(FIRST, send, own, (start,), weight)
    current, applied, direction, send, own = apply("first", gram=gram, vectors=(start, product, weight))
    product, gram = gather(LATER, send, own, (applied, direction, current), weight)
    current, applied, direction, send, own = apply(
        "later", gram=gram, vectors=(current, applied, direction, product, weight)
    )
    product, gram = gather(LAST, send, own, (applied, direction, current), None)
    state, energy = finish(entries, gram, current, direction)
    return (state[None], energy[0, :1])


def solution(mesh):
    in_specs = (
        P("seg", "sec", None, None),
        P("seg", "sec", None, None),
        P("seg", "sec", None, None),
        P("seg", "sec", None, None),
        P("seg", "sec", None, None),
        P(),
        P(),
        P(),
        P(),
        P(),
    )
    out_specs = (P("seg", "sec", None, None), P("seg"))
    return jax.shard_map(
        on_device, mesh=mesh, in_specs=in_specs, out_specs=out_specs, check_vma=False
    )
```

```python
import functools

import jax
import jax.numpy as jnp
from jax import lax
from jax.experimental import pallas as pl
from jax.experimental.pallas import tpu as pltpu
from jax.sharding import PartitionSpec as P

W = 30
D = 4
B = 64
SEC_DEV = 8
CLASSES = 5
GROUP = W // CLASSES
PAIRS = SEC_DEV * CLASSES
HALF = B // 2
FOLD = 2 * B
ROWS = W * HALF
TILE = D * HALF
MIX = 128
PITCH = 33
EPSILON = 1e-06
BF = jnp.bfloat16
F32 = jnp.float32


def passed_along(block, axis, distance):
    devices = range(lax.axis_size(axis))
    route = [(i - distance, i) for i in devices if i - distance in devices]
    return lax.ppermute(block, axis, route)


def low_lanes(rows):
    return lax.broadcasted_iota(jnp.int32, (rows, FOLD), 1) < B


def fold_pair(pair):
    stacked = jnp.concatenate([pair, pltpu.roll(pair, FOLD - HALF, 1)], axis=0)
    turned = stacked.T
    return turned[:HALF], turned[B : B + HALF]


def unfold_pair(first, second):
    filler = jnp.zeros((HALF, FOLD), F32)
    turned = jnp.concatenate([first, filler, second, filler], axis=0).T
    upper = lax.broadcasted_iota(jnp.int32, (B, FOLD), 1) % B < HALF
    return jnp.where(upper, turned[:B], pltpu.roll(turned[B:], HALF, 1))


def spread(tile):
    rolled = pltpu.roll(tile, B, 1)
    low = low_lanes(HALF)
    zero = jnp.zeros_like(tile)
    return jnp.concatenate(
        [
            jnp.where(low, tile, zero),
            jnp.where(low, rolled, zero),
            jnp.where(low, zero, rolled),
            jnp.where(low, zero, tile),
        ],
        axis=0,
    )


def spread_pair(pair):
    rolled = pltpu.roll(pair, B, 1)
    low = low_lanes(B)
    zero = jnp.zeros_like(pair)
    first = jnp.concatenate([jnp.where(low, pair, zero), jnp.where(low, zero, rolled)], axis=0)
    second = jnp.concatenate([jnp.where(low, rolled, zero), jnp.where(low, zero, pair)], axis=0)
    return first, second


def dot(left, right):
    return jnp.dot(left, right, preferred_element_type=F32)


def route_kernel(me_ref, shift_ref, site_ref, slot_ref, local_ref, take_ref, send_ref, count, source):
    groups = send_ref.shape[0]
    slots = send_ref.shape[1]
    me = me_ref[0]
    for g in range(groups):
        count[g] = 0
    for i in range(groups * slots):
        source[i] = 0
    for l in range(SEC_DEV):
        for k in range(CLASSES):
            target = shift_ref[k, me * SEC_DEV + l]
            owner = target // SEC_DEV
            rank = count[owner]
            count[owner] = rank + 1
            slot = owner * slots + jnp.minimum(rank, slots - 1)
            slot_ref[l * CLASSES + k] = jnp.where(owner == me, -1, slot)
            local_ref[l * CLASSES + k] = target % SEC_DEV

    def one_group(g, carry):
        rank = jnp.int32(0)
        for l in range(SEC_DEV):
            for k in range(CLASSES):
                target = shift_ref[k, g * SEC_DEV + l]
                hit = target // SEC_DEV == me
                place = jnp.minimum(rank, slots - 1)

                @pl.when(hit)
                def _():
                    local = target % SEC_DEV
                    take_ref[k * SEC_DEV + local] = jnp.where(g == me, -1, g * slots + place)
                    source[g * slots + place] = local

                rank = rank + hit.astype(jnp.int32)
        return carry

    lax.fori_loop(0, groups, one_group, 0)

    def one_copy(g, carry):
        for r in range(slots):
            send_ref[g, r] = site_ref[source[g * slots + r]]
        return carry

    lax.fori_loop(0, groups, one_copy, 0)


def route(me, sector_shift, site, groups, slots):
    smem = pl.BlockSpec(memory_space=pltpu.SMEM)
    vmem = pl.BlockSpec(memory_space=pltpu.VMEM)
    return pl.pallas_call(
        route_kernel,
        out_shape=(
            jax.ShapeDtypeStruct((PAIRS,), jnp.int32),
            jax.ShapeDtypeStruct((PAIRS,), jnp.int32),
            jax.ShapeDtypeStruct((PAIRS,), jnp.int32),
            jax.ShapeDtypeStruct((groups, slots, B, D * B), BF),
        ),
        in_specs=[smem, smem, vmem],
        out_specs=(smem, smem, smem, vmem),
        scratch_shapes=[pltpu.SMEM((groups,), jnp.int32), pltpu.SMEM((groups * slots,), jnp.int32)],
        name="route",
    )(me, sector_shift, site)


def fold_environment_kernel(in_ref, out_ref):
    for i in range(W // 2):
        pair = in_ref[0, :, i * FOLD : (i + 1) * FOLD].astype(F32)
        first, second = fold_pair(pair)
        out_ref[0, (2 * i) * HALF : (2 * i + 1) * HALF, :] = first.astype(BF)
        out_ref[0, (2 * i + 1) * HALF : (2 * i + 2) * HALF, :] = second.astype(BF)


def fold_environment(environment):
    return pl.pallas_call(
        fold_environment_kernel,
        grid=(SEC_DEV,),
        out_shape=jax.ShapeDtypeStruct((SEC_DEV, ROWS, FOLD), BF),
        in_specs=[pl.BlockSpec((1, B, W * B), lambda l: (l, 0, 0))],
        out_specs=pl.BlockSpec((1, ROWS, FOLD), lambda l: (l, 0, 0)),
        name="fold_environment",
        cost_estimate=pl.CostEstimate(flops=0, bytes_accessed=4 * SEC_DEV * ROWS * FOLD, transcendentals=0),
    )(environment)


def live_mask(left_size, right_sizes):
    half_p = lax.broadcasted_iota(jnp.int32, (HALF, FOLD), 1)
    column = lax.broadcasted_iota(jnp.int32, (HALF, FOLD), 0) + jnp.where(half_p < B, 0, HALF)
    row = jnp.where(half_p < B, half_p, half_p - B)
    parts = [
        jnp.where((row < left_size) & (column < right_sizes[t]), 1.0, 0.0).astype(F32) for t in range(D)
    ]
    return jnp.concatenate(parts, axis=0)


def fold_state_kernel(left_ref, right_ref, state_ref, weight_ref, start_ref, fold_ref):
    l = pl.program_id(0)
    mask = live_mask(left_ref[l], [right_ref[l * D + t] for t in range(D)])
    for source, result in ((state_ref, start_ref), (weight_ref, fold_ref)):
        tiles = []
        for i in range(D // 2):
            tiles.extend(fold_pair(source[0, :, i * FOLD : (i + 1) * FOLD]))
        folded = jnp.concatenate(tiles, axis=0)
        result[0] = mask * folded if result is start_ref else folded


def fold_state(left_sizes, right_sizes, state, weight):
    natural = pl.BlockSpec((1, B, D * B), lambda l, *refs: (l, 0, 0))
    folded = pl.BlockSpec((1, TILE, FOLD), lambda l, *refs: (l, 0, 0))
    shape = jax.ShapeDtypeStruct((SEC_DEV, TILE, FOLD), F32)
    return pl.pallas_call(
        fold_state_kernel,
        out_shape=(shape, shape),
        grid_spec=pltpu.PrefetchScalarGridSpec(
            num_scalar_prefetch=2,
            grid=(SEC_DEV,),
            in_specs=[natural, natural],
            out_specs=(folded, folded),
        ),
        name="fold_state",
        cost_estimate=pl.CostEstimate(flops=0, bytes_accessed=16 * SEC_DEV * TILE * FOLD, transcendentals=0),
    )(left_sizes, right_sizes, state, weight)


def mix_channels(mix, first, second):
    for j in range(0, HALF, 2):
        parts = [first[pl.ds(j + i, MIX, stride=PITCH), :].astype(BF) for i in range(2)]
        mixed = dot(mix, jnp.concatenate(parts, axis=1))
        for i in range(2):
            second[pl.ds(j + i, MIX, stride=PITCH), :] = mixed[:, i * FOLD : (i + 1) * FOLD]


def mixed_rows(ref, x):
    return jnp.concatenate(
        [ref[(x * D + y) * PITCH : (x * D + y) * PITCH + HALF, :].astype(BF) for y in range(D)], axis=0
    )


def build_kernel(slot_ref, local_ref, env_ref, own_ref, came_ref, mix_ref, out_ref, first, second):
    l = pl.program_id(0)

    @pl.when(l == 0)
    def _():
        first[W * D * PITCH :, :] = jnp.zeros(((MIX - W * D) * PITCH, FOLD), F32)

    mix_turned = mix_ref[...].astype(F32).T.astype(BF)
    for k in range(CLASSES):
        slot = slot_ref[l * CLASSES + k]
        local = local_ref[l * CLASSES + k]
        tensor = jnp.where(slot < 0, own_ref[local], came_ref[jnp.maximum(slot, 0)])
        blocks = []
        for i in range(D // 2):
            blocks.extend(spread_pair(tensor[:, i * FOLD : (i + 1) * FOLD].astype(F32)))
        right = jnp.concatenate(blocks, axis=1).astype(BF)
        left = env_ref[0, k * GROUP * HALF : (k + 1) * GROUP * HALF, :]
        joined = dot(left, right)
        for j in range(GROUP):
            for t in range(D):
                at = ((k * GROUP + j) * D + t) * PITCH
                first[at : at + HALF, :] = joined[j * HALF : (j + 1) * HALF, t * FOLD : (t + 1) * FOLD]
    mix_channels(mix_turned, first, second)
    own = own_ref[l]
    tiles = []
    low_half = low_lanes(HALF)
    for i in range(D // 2):
        pair = own[:, i * FOLD : (i + 1) * FOLD].astype(F32)
        rolled = pltpu.roll(pair, B, 1)
        tiles.append(jnp.where(low_half, pair[:HALF], rolled[HALF:]))
        tiles.append(jnp.where(low_half, rolled[:HALF], pair[HALF:]))
    turned = jnp.concatenate(tiles, axis=0).T.astype(BF)
    low = low_lanes(B)
    for v in range(0, W, 2):
        right = jnp.concatenate(
            [mixed_rows(second, v + i) for i in range(2)], axis=1
        )
        product = dot(turned, right)
        for i in range(2):
            block = product[:, i * FOLD : (i + 1) * FOLD]
            chosen = jnp.where(low, block[:B], block[B:])
            total = chosen + pltpu.roll(chosen, B, 1)
            folded = jnp.where(low_half, total[:HALF], total[HALF:])
            out_ref[0, (v + i) * HALF : (v + i + 1) * HALF, :] = folded.astype(BF)


def build_environment(slot, local, environment, site, came, mix):
    folded = pl.BlockSpec((1, ROWS, FOLD), lambda l, *refs: (l, 0, 0))
    whole = lambda shape: pl.BlockSpec(shape, lambda l, *refs: (0,) * len(shape))
    return pl.pallas_call(
        build_kernel,
        out_shape=jax.ShapeDtypeStruct((SEC_DEV, ROWS, FOLD), BF),
        grid_spec=pltpu.PrefetchScalarGridSpec(
            num_scalar_prefetch=2,
            grid=(SEC_DEV,),
            in_specs=[folded, whole(site.shape), whole(came.shape), whole(mix.shape)],
            out_specs=folded,
            scratch_shapes=[pltpu.VMEM((MIX * PITCH, FOLD), F32), pltpu.VMEM((MIX * PITCH, FOLD), F32)],
        ),
        name="build_environment",
        cost_estimate=pl.CostEstimate(flops=10**10, bytes_accessed=10**7, transcendentals=0),
    )(slot, local, environment, site, came, mix)


def gram_sums(gram_ref, entries):
    total = gram_ref[0]
    for g in range(1, gram_ref.shape[0]):
        total = total + gram_ref[g]
    row = total[:1] * (1.0 / entries)
    lane = lax.broadcasted_iota(jnp.int32, (1, FOLD), 1)
    return lambda i: jnp.sum(jnp.where(lane == i, row, 0.0), axis=1, keepdims=True)


def rotation(cross_sum, far, rayleigh_value):
    up, along = -cross_sum, far - rayleigh_value
    scale = jnp.maximum(jnp.abs(up), jnp.abs(along))
    flat = scale == 0.0
    scale = jnp.where(flat, 1.0, scale)
    up, along = up / scale, along / scale
    length = jnp.sqrt(up * up + along * along)
    length = jnp.where(flat, 1.0, length)
    larger = jnp.sqrt(0.5 * (1.0 + jnp.abs(along) / length))
    smaller = jnp.abs(up) / (2.0 * length * larger)
    ahead = along >= 0.0
    cosine = jnp.where(flat, 1.0, jnp.where(ahead, larger, smaller))
    size = jnp.where(ahead, smaller, larger)
    sine = jnp.where(flat, 0.0, jnp.where(cross_sum < 0.0, size, -size))
    return cosine, sine


def correction_scalars(xx, xa, xpa, xpx, papa, papx, pxpx):
    along = xpa - xa * xpx
    square = papa - 2.0 * xa * papx + xa * xa * pxpx
    square = square - 2.0 * along * along + along * along * xx
    return xa, along, lax.rsqrt(jnp.maximum(square, 0.0) + EPSILON)


FIRST = ("uu", "uh", "uPh", "uPu", "PhPh", "PhPu", "PuPu")
LATER = (
    "xx", "xd", "dd", "xa", "xp", "da", "dp", "xPa", "xPp", "dPa", "dPp", "xPx", "xPd", "dPd",
    "PaPa", "PaPp", "PpPp", "PaPx", "PaPd", "PpPx", "PpPd", "PxPx", "PxPd", "PdPd",
)
LAST = ("xa", "xp", "da", "dp")


def split_name(name):
    parts, at = [], 0
    while at < len(name):
        size = 2 if name[at] == "P" else 1
        parts.append(name[at : at + size])
        at += size
    return parts


def first_scalars(gram_ref, entries):
    sums = gram_sums(gram_ref, entries)
    value = {name: sums(i) for i, name in enumerate(FIRST)}
    inverse = lax.rsqrt(value["uu"] + EPSILON)
    square = inverse * inverse
    named = [value[name] * square for name in FIRST]
    return (inverse,) + correction_scalars(*named)


def later_scalars(gram_ref, entries):
    sums = gram_sums(gram_ref, entries)
    value = {name: sums(i) for i, name in enumerate(LATER)}
    cosine, sine = rotation(value["xp"] + value["da"], value["dp"], value["xa"])
    cc, cs, ss = cosine * cosine, cosine * sine, sine * sine

    def turned(a, b, c, d):
        return cc * value[a] + cs * (value[b] + value[c]) + ss * value[d]

    named = (
        turned("xx", "xd", "xd", "dd"),
        turned("xa", "xp", "da", "dp"),
        turned("xPa", "xPp", "dPa", "dPp"),
        turned("xPx", "xPd", "xPd", "dPd"),
        turned("PaPa", "PaPp", "PaPp", "PpPp"),
        turned("PaPx", "PaPd", "PpPx", "PpPd"),
        turned("PxPx", "PxPd", "PxPd", "PdPd"),
    )
    return (cosine, sine) + correction_scalars(*named)


def apply_kernel(mode, entries, *refs):
    slot_ref, local_ref, mix_ref, right_ref, left_ref = refs[:5]
    refs = refs[5:]
    l = pl.program_id(0)
    if mode == "start":
        state_ref, send_ref, own_ref, first, second, fixed = refs
    elif mode == "first":
        gram_ref, u_ref, h_ref, weight_ref = refs[:4]
        x_out, a_out, d_out, send_ref, own_ref, first, second, fixed = refs[4:]
    else:
        gram_ref, x_ref, a_ref, d_ref, p_ref, weight_ref = refs[:6]
        x_out, a_out, d_out, send_ref, own_ref, first, second, fixed = refs[6:]

    @pl.when(l == 0)
    def _():
        own_ref[...] = jnp.zeros_like(own_ref)
        first[W * D * PITCH :, :] = jnp.zeros(((MIX - W * D) * PITCH, FOLD), F32)
        if mode != "start":
            scalars = first_scalars if mode == "first" else later_scalars
            for i, value in enumerate(scalars(gram_ref, entries)):
                fixed[i : i + 1, :] = jnp.broadcast_to(value, (1, FOLD))

    if mode == "start":
        vector = state_ref[0]
    else:
        if mode == "first":
            inverse, rho, along, norm = [fixed[i : i + 1, :] for i in range(4)]
            current = inverse * u_ref[0]
            applied = inverse * h_ref[0]
        else:
            cosine, sine, rho, along, norm = [fixed[i : i + 1, :] for i in range(5)]
            current = cosine * x_ref[0] + sine * d_ref[0]
            applied = cosine * a_ref[0] + sine * p_ref[0]
        vector = (weight_ref[0] * (applied - rho * current) - along * current) * norm
        x_out[0] = current
        a_out[0] = applied
        d_out[0] = vector

    right = jnp.concatenate(
        [spread(vector[s * HALF : (s + 1) * HALF]) for s in range(D)], axis=1
    ).astype(BF)
    step = GROUP * HALF
    for i in range(CLASSES):
        product = dot(right_ref[0, i * step : (i + 1) * step, :], right)
        for v in range(GROUP):
            for s in range(D):
                at = ((i * GROUP + v) * D + s) * PITCH
                first[at : at + HALF, :] = product[v * HALF : (v + 1) * HALF, s * FOLD : (s + 1) * FOLD]
    mix_channels(mix_ref[...], first, second)
    for k in range(CLASSES):
        rows, blocks = [], []
        for w in range(k * GROUP, (k + 1) * GROUP):
            rows.append(mixed_rows(second, w))
            blocks.append(spread(left_ref[0, w * HALF : (w + 1) * HALF, :].astype(F32)).astype(BF))
        partial = dot(jnp.concatenate(rows, axis=1), jnp.concatenate(blocks, axis=0))
        slot = slot_ref[l * CLASSES + k]
        local = local_ref[l * CLASSES + k]

        @pl.when(slot >= 0)
        def _():
            send_ref[jnp.maximum(slot, 0)] = partial.astype(BF)

        @pl.when(slot < 0)
        def _():
            own_ref[local] = own_ref[local] + partial


def apply_operator(mode, entries, slots_total, slot, local, mix, right_env, left_env, gram, vectors):
    vector = pl.BlockSpec((1, TILE, FOLD), lambda l, *refs: (l, 0, 0))
    folded = pl.BlockSpec((1, ROWS, FOLD), lambda l, *refs: (l, 0, 0))
    whole = lambda shape: pl.BlockSpec(shape, lambda l, *refs: (0,) * len(shape))
    shape = jax.ShapeDtypeStruct((SEC_DEV, TILE, FOLD), F32)
    kept = 0 if mode == "start" else 3
    send = jax.ShapeDtypeStruct((slots_total, TILE, FOLD), BF)
    inputs = (mix, right_env, left_env) + (() if gram is None else (gram,)) + tuple(vectors)
    return pl.pallas_call(
        functools.partial(apply_kernel, mode, entries),
        out_shape=(shape,) * kept + (send, shape),
        grid_spec=pltpu.PrefetchScalarGridSpec(
            num_scalar_prefetch=2,
            grid=(SEC_DEV,),
            in_specs=[whole(mix.shape), folded, folded]
            + ([] if gram is None else [whole(gram.shape)])
            + [vector] * len(vectors),
            out_specs=(vector,) * kept + (whole(send.shape), whole(shape.shape)),
            scratch_shapes=[
                pltpu.VMEM((MIX * PITCH, FOLD), F32),
                pltpu.VMEM((MIX * PITCH, FOLD), F32),
                pltpu.VMEM((8, FOLD), F32),
            ],
        ),
        name="apply_" + mode,
        cost_estimate=pl.CostEstimate(flops=10**10, bytes_accessed=10**7, transcendentals=0),
    )(slot, local, *inputs)


def collect_kernel(names, *refs):
    take_ref, left_ref, right_ref = refs[:3]
    came_ref, own_ref = refs[3:5]
    symbols = sorted({part[-1] for name in names for part in split_name(name)} - {"h", "p"})
    weighted = any("P" in name for name in names)
    vectors = refs[5 : 5 + len(symbols)]
    at = 5 + len(symbols)
    weight_ref = None
    if weighted:
        weight_ref = refs[at]
        at += 1
    out_ref, gram_ref, sums = refs[at:]
    result = "h" if names is FIRST else "p"
    m = pl.program_id(0)

    @pl.when(m == 0)
    def _():
        sums[...] = jnp.zeros_like(sums)

    total = own_ref[0]
    for k in range(CLASSES):
        place = take_ref[k * SEC_DEV + m]
        part = came_ref[jnp.maximum(place, 0)].astype(F32)
        total = total + jnp.where(place >= 0, part, 0.0)
    total = live_mask(left_ref[m], [right_ref[m * D + t] for t in range(D)]) * total
    out_ref[0] = total
    size = 8
    totals = [jnp.zeros((size, FOLD), F32) for name in names]
    for i in range(TILE // size):
        rows = slice(i * size, (i + 1) * size)
        value = {symbol: ref[0, rows, :] for symbol, ref in zip(symbols, vectors)}
        value[result] = total[rows]
        if weighted:
            weight = weight_ref[0, rows, :]
            for symbol in list(value):
                value["P" + symbol] = weight * value[symbol]
        for n, name in enumerate(names):
            one, two = split_name(name)
            totals[n] = totals[n] + value[one] * value[two]
    for n in range(len(names)):
        sums[n] = sums[n] + totals[n]

    @pl.when(m == SEC_DEV - 1)
    def _():
        lane = lax.broadcasted_iota(jnp.int32, (8, FOLD), 1)
        packed = jnp.zeros((8, FOLD), F32)
        for n in range(len(names)):
            packed = jnp.where(lane == n, jnp.sum(sums[n], keepdims=True), packed)
        for g in range(gram_ref.shape[0]):
            gram_ref[g] = packed


def collect(names, groups, take, left_sizes, right_sizes, came, own, vectors, weight):
    vector = pl.BlockSpec((1, TILE, FOLD), lambda m, *refs: (m, 0, 0))
    whole = lambda shape: pl.BlockSpec(shape, lambda m, *refs: (0,) * len(shape))
    extra = () if weight is None else (weight,)
    gram = jax.ShapeDtypeStruct((groups, 8, FOLD), F32)
    return pl.pallas_call(
        functools.partial(collect_kernel, names),
        out_shape=(jax.ShapeDtypeStruct((SEC_DEV, TILE, FOLD), F32), gram),
        grid_spec=pltpu.PrefetchScalarGridSpec(
            num_scalar_prefetch=3,
            grid=(SEC_DEV,),
            in_specs=[whole(came.shape)] + [vector] * (1 + len(vectors) + len(extra)),
            out_specs=(vector, whole(gram.shape)),
            scratch_shapes=[pltpu.VMEM((len(names), 8, FOLD), F32)],
        ),
        name="collect",
        cost_estimate=pl.CostEstimate(flops=10**7, bytes_accessed=4 * 10**6, transcendentals=0),
    )(take, left_sizes, right_sizes, came, own, *vectors, *extra)


def finish_kernel(entries, gram_ref, x_ref, d_ref, state_ref, energy_ref, fixed):
    l = pl.program_id(0)

    @pl.when(l == 0)
    def _():
        sums = gram_sums(gram_ref, entries)
        xa, xp, da, dp = [sums(i) for i in range(4)]
        cosine, sine = rotation(xp + da, dp, xa)
        energy = cosine * cosine * xa + cosine * sine * (xp + da) + sine * sine * dp
        fixed[0:1, :] = jnp.broadcast_to(cosine, (1, FOLD))
        fixed[1:2, :] = jnp.broadcast_to(sine, (1, FOLD))
        energy_ref[...] = jnp.broadcast_to(energy, energy_ref.shape)

    final = fixed[0:1, :] * x_ref[0] + fixed[1:2, :] * d_ref[0]
    for i in range(D // 2):
        first = final[(2 * i) * HALF : (2 * i + 1) * HALF]
        second = final[(2 * i + 1) * HALF : (2 * i + 2) * HALF]
        state_ref[0, :, i * FOLD : (i + 1) * FOLD] = unfold_pair(first, second)


def finish(entries, gram, current, direction):
    vector = pl.BlockSpec((1, TILE, FOLD), lambda l: (l, 0, 0))
    return pl.pallas_call(
        functools.partial(finish_kernel, entries),
        grid=(SEC_DEV,),
        out_shape=(
            jax.ShapeDtypeStruct((SEC_DEV, B, D * B), F32),
            jax.ShapeDtypeStruct((8, FOLD), F32),
        ),
        in_specs=[pl.BlockSpec(gram.shape, lambda l: (0, 0, 0)), vector, vector],
        out_specs=(
            pl.BlockSpec((1, B, D * B), lambda l: (l, 0, 0)),
            pl.BlockSpec((8, FOLD), lambda l: (0, 0)),
        ),
        scratch_shapes=[pltpu.VMEM((8, FOLD), F32)],
        name="finish",
        cost_estimate=pl.CostEstimate(flops=10**6, bytes_accessed=2 * 10**6, transcendentals=0),
    )(gram, current, direction)


def exchange(blocks):
    return lax.all_to_all(blocks, "sec", 0, 0, tiled=True)


def on_device(
    left_environment,
    right_environment,
    site_previous,
    state_start,
    preconditioner,
    channel_tensor,
    channel_mask,
    sector_shift,
    left_sizes,
    right_sizes,
):
    groups = lax.axis_size("sec")
    my_group = lax.axis_index("sec")
    offset = my_group * SEC_DEV
    slots = (PAIRS + groups - 1) // groups
    entries = float(SEC_DEV * B * D * B * groups)
    my_left = lax.dynamic_slice_in_dim(left_sizes, offset, SEC_DEV, 0)
    my_right = lax.dynamic_slice_in_dim(right_sizes, offset, SEC_DEV, 0).reshape(SEC_DEV * D)
    position = lax.axis_index("seg")
    last = lax.axis_size("seg") - 1

    came_right = passed_along(right_environment[0], "seg", -1)
    right_used = jnp.where(position == last, right_environment[0], came_right)

    slot, local, take, site_send = route(my_group[None], sector_shift, site_previous[0], groups, slots)
    site_came = exchange(site_send).reshape(groups * slots, B, D * B)
    mix = channel_tensor * channel_mask.astype(BF)[:, None, :, None]
    mix = jnp.pad(mix.reshape(W * D, W * D), ((0, MIX - W * D), (0, MIX - W * D)))

    own_left = fold_environment(left_environment[0])
    fresh = build_environment(slot, local, own_left, site_previous[0], site_came, mix)
    handed = passed_along(fresh, "seg", 1)
    left_env = jnp.where(position == 0, own_left, handed)
    right_env = fold_environment(right_used)
    start, weight = fold_state(my_left, my_right, state_start[0], preconditioner[0])

    apply = functools.partial(
        apply_operator, entries=entries, slots_total=groups * slots, slot=slot, local=local, mix=mix,
        right_env=right_env, left_env=left_env,
    )

    def gather(names, send, own, vectors, weight):
        came = exchange(send.reshape(groups, slots, TILE, FOLD)).reshape(groups * slots, TILE, FOLD)
        result, gram = collect(names, groups, take, my_left, my_right, came, own, vectors, weight)
        return result, exchange(gram)

    send, own = apply("start", gram=None, vectors=(start,))
    product, gram = gather(FIRST, send, own, (start,), weight)
    current, applied, direction, send, own = apply("first", gram=gram, vectors=(start, product, weight))
    product, gram = gather(LATER, send, own, (applied, direction, current), weight)
    current, applied, direction, send, own = apply(
        "later", gram=gram, vectors=(current, applied, direction, product, weight)
    )
    product, gram = gather(LAST, send, own, (applied, direction, current), None)
    state, energy = finish(entries, gram, current, direction)
    return (state[None], energy[0, :1])


def solution(mesh):
    in_specs = (
        P("seg", "sec", None, None),
        P("seg", "sec", None, None),
        P("seg", "sec", None, None),
        P("seg", "sec", None, None),
        P("seg", "sec", None, None),
        P(),
        P(),
        P(),
        P(),
        P(),
    )
    out_specs = (P("seg", "sec", None, None), P("seg"))
    return jax.shard_map(
        on_device, mesh=mesh, in_specs=in_specs, out_specs=out_specs, check_vma=False
    )
```

```python
import functools

import jax
import jax.numpy as jnp
from jax import lax
from jax.experimental import pallas as pl
from jax.experimental.pallas import tpu as pltpu
from jax.sharding import PartitionSpec as P

W = 30
D = 4
B = 64
SEC_DEV = 8
CLASSES = 5
GROUP = W // CLASSES
PAIRS = SEC_DEV * CLASSES
HALF = B // 2
FOLD = 2 * B
ROWS = W * HALF
TILE = D * HALF
MIX = 128
PITCH = 33
EPSILON = 1e-06
BF = jnp.bfloat16
F32 = jnp.float32


def passed_along(block, axis, distance):
    devices = range(lax.axis_size(axis))
    route = [(i - distance, i) for i in devices if i - distance in devices]
    return lax.ppermute(block, axis, route)


def low_lanes(rows):
    return lax.broadcasted_iota(jnp.int32, (rows, FOLD), 1) < B


def fold_pair(pair):
    stacked = jnp.concatenate([pair, pltpu.roll(pair, FOLD - HALF, 1)], axis=0)
    turned = stacked.T
    return turned[:HALF], turned[B : B + HALF]


def unfold_pair(first, second):
    filler = jnp.zeros((HALF, FOLD), F32)
    turned = jnp.concatenate([first, filler, second, filler], axis=0).T
    upper = lax.broadcasted_iota(jnp.int32, (B, FOLD), 1) % B < HALF
    return jnp.where(upper, turned[:B], pltpu.roll(turned[B:], HALF, 1))


def spread(tile):
    rolled = pltpu.roll(tile, B, 1)
    low = low_lanes(HALF)
    zero = jnp.zeros_like(tile)
    return jnp.concatenate(
        [
            jnp.where(low, tile, zero),
            jnp.where(low, rolled, zero),
            jnp.where(low, zero, rolled),
            jnp.where(low, zero, tile),
        ],
        axis=0,
    )


def spread_pair(pair):
    rolled = pltpu.roll(pair, B, 1)
    low = low_lanes(B)
    zero = jnp.zeros_like(pair)
    first = jnp.concatenate([jnp.where(low, pair, zero), jnp.where(low, zero, rolled)], axis=0)
    second = jnp.concatenate([jnp.where(low, rolled, zero), jnp.where(low, zero, pair)], axis=0)
    return first, second


def dot(left, right):
    return jnp.dot(left, right, preferred_element_type=F32)


def route_kernel(me_ref, shift_ref, site_ref, slot_ref, local_ref, take_ref, send_ref, count, source):
    groups = send_ref.shape[0]
    slots = send_ref.shape[1]
    me = me_ref[0]
    for g in range(groups):
        count[g] = 0
    for i in range(groups * slots):
        source[i] = 0
    for l in range(SEC_DEV):
        for k in range(CLASSES):
            target = shift_ref[k, me * SEC_DEV + l]
            owner = target // SEC_DEV
            rank = count[owner]
            count[owner] = rank + 1
            slot_ref[l * CLASSES + k] = owner * slots + jnp.minimum(rank, slots - 1)
            local_ref[l * CLASSES + k] = jnp.where(owner == me, target % SEC_DEV, -1)

    def one_group(g, carry):
        rank = jnp.int32(0)
        for l in range(SEC_DEV):
            for k in range(CLASSES):
                target = shift_ref[k, g * SEC_DEV + l]
                hit = target // SEC_DEV == me
                place = jnp.minimum(rank, slots - 1)

                @pl.when(hit)
                def _():
                    local = target % SEC_DEV
                    take_ref[k * SEC_DEV + local] = jnp.where(g == me, -1, g * slots + place)
                    source[g * slots + place] = local

                rank = rank + hit.astype(jnp.int32)
        return carry

    lax.fori_loop(0, groups, one_group, 0)

    def one_copy(g, carry):
        for r in range(slots):
            send_ref[g, r] = site_ref[source[g * slots + r]]
        return carry

    lax.fori_loop(0, groups, one_copy, 0)


def route(me, sector_shift, site, groups, slots):
    smem = pl.BlockSpec(memory_space=pltpu.SMEM)
    vmem = pl.BlockSpec(memory_space=pltpu.VMEM)
    return pl.pallas_call(
        route_kernel,
        out_shape=(
            jax.ShapeDtypeStruct((PAIRS,), jnp.int32),
            jax.ShapeDtypeStruct((PAIRS,), jnp.int32),
            jax.ShapeDtypeStruct((PAIRS,), jnp.int32),
            jax.ShapeDtypeStruct((groups, slots, B, D * B), BF),
        ),
        in_specs=[smem, smem, vmem],
        out_specs=(smem, smem, smem, vmem),
        scratch_shapes=[pltpu.SMEM((groups,), jnp.int32), pltpu.SMEM((groups * slots,), jnp.int32)],
        name="route",
    )(me, sector_shift, site)


def fold_environment_kernel(flag_ref, *refs):
    out_ref = refs[-1]
    for n in range(out_ref.shape[0]):
        for i in range(W // 2):
            pairs = [ref[n, :, i * FOLD : (i + 1) * FOLD].astype(F32) for ref in refs[:-1]]
            pair = pairs[0] if len(pairs) == 1 else jnp.where(flag_ref[0] == 1, pairs[0], pairs[1])
            first, second = fold_pair(pair)
            out_ref[n, (2 * i) * HALF : (2 * i + 1) * HALF, :] = first.astype(BF)
            out_ref[n, (2 * i + 1) * HALF : (2 * i + 2) * HALF, :] = second.astype(BF)


def fold_environment(flag, *environments):
    step = 2
    return pl.pallas_call(
        fold_environment_kernel,
        out_shape=jax.ShapeDtypeStruct((SEC_DEV, ROWS, FOLD), BF),
        grid_spec=pltpu.PrefetchScalarGridSpec(
            num_scalar_prefetch=1,
            grid=(SEC_DEV // step,),
            in_specs=[pl.BlockSpec((step, B, W * B), lambda l, *refs: (l, 0, 0))] * len(environments),
            out_specs=pl.BlockSpec((step, ROWS, FOLD), lambda l, *refs: (l, 0, 0)),
        ),
        name="fold_environment",
        cost_estimate=pl.CostEstimate(
            flops=0, bytes_accessed=4 * SEC_DEV * ROWS * FOLD, transcendentals=0
        ),
    )(flag, *environments)


def live_mask(left_size, right_sizes):
    half_p = lax.broadcasted_iota(jnp.int32, (HALF, FOLD), 1)
    column = lax.broadcasted_iota(jnp.int32, (HALF, FOLD), 0) + jnp.where(half_p < B, 0, HALF)
    row = jnp.where(half_p < B, half_p, half_p - B)
    parts = [
        jnp.where((row < left_size) & (column < right_sizes[t]), 1.0, 0.0).astype(F32) for t in range(D)
    ]
    return jnp.concatenate(parts, axis=0)


def fold_state_kernel(left_ref, right_ref, state_ref, weight_ref, start_ref, fold_ref):
    for n in range(state_ref.shape[0]):
        l = pl.program_id(0) * state_ref.shape[0] + n
        mask = live_mask(left_ref[l], [right_ref[l * D + t] for t in range(D)])
        for source, result in ((state_ref, start_ref), (weight_ref, fold_ref)):
            tiles = []
            for i in range(D // 2):
                tiles.extend(fold_pair(source[n, :, i * FOLD : (i + 1) * FOLD]))
            folded = jnp.concatenate(tiles, axis=0)
            result[n] = mask * folded if result is start_ref else folded


def fold_state(left_sizes, right_sizes, state, weight):
    step = 4
    natural = pl.BlockSpec((step, B, D * B), lambda l, *refs: (l, 0, 0))
    folded = pl.BlockSpec((step, TILE, FOLD), lambda l, *refs: (l, 0, 0))
    shape = jax.ShapeDtypeStruct((SEC_DEV, TILE, FOLD), F32)
    return pl.pallas_call(
        fold_state_kernel,
        out_shape=(shape, shape),
        grid_spec=pltpu.PrefetchScalarGridSpec(
            num_scalar_prefetch=2,
            grid=(SEC_DEV // step,),
            in_specs=[natural, natural],
            out_specs=(folded, folded),
        ),
        name="fold_state",
        cost_estimate=pl.CostEstimate(flops=0, bytes_accessed=16 * SEC_DEV * TILE * FOLD, transcendentals=0),
    )(left_sizes, right_sizes, state, weight)


def mix_channels(mix, first, second):
    for j in range(0, HALF, 2):
        parts = [first[pl.ds(j + i, MIX, stride=PITCH), :].astype(BF) for i in range(2)]
        mixed = dot(mix, jnp.concatenate(parts, axis=1))
        for i in range(2):
            second[pl.ds(j + i, MIX, stride=PITCH), :] = mixed[:, i * FOLD : (i + 1) * FOLD]


def mixed_rows(ref, x):
    return jnp.concatenate(
        [ref[(x * D + y) * PITCH : (x * D + y) * PITCH + HALF, :].astype(BF) for y in range(D)], axis=0
    )


def build_kernel(half, slot_ref, local_ref, env_ref, own_ref, came_ref, mix_ref, out_ref, *scratch):
    size = env_ref.shape[0]
    base = half + pl.program_id(0) * size

    @pl.when(pl.program_id(0) == 0)
    def _():
        for first in scratch[:size]:
            first[W * D * PITCH :, :] = jnp.zeros(((MIX - W * D) * PITCH, FOLD), F32)

    mix_turned = mix_ref[...].astype(F32).T.astype(BF)
    for n in range(size):
        first = scratch[n]
        for k in range(CLASSES):
            slot = slot_ref[(base + n) * CLASSES + k]
            local = local_ref[(base + n) * CLASSES + k]
            tensor = jnp.where(local >= 0, own_ref[jnp.maximum(local, 0)], came_ref[slot])
            blocks = []
            for i in range(D // 2):
                blocks.extend(spread_pair(tensor[:, i * FOLD : (i + 1) * FOLD].astype(F32)))
            right = jnp.concatenate(blocks, axis=1).astype(BF)
            left = env_ref[n, k * GROUP * HALF : (k + 1) * GROUP * HALF, :]
            joined = dot(left, right)
            for j in range(GROUP):
                for t in range(D):
                    at = ((k * GROUP + j) * D + t) * PITCH
                    first[at : at + HALF, :] = joined[j * HALF : (j + 1) * HALF, t * FOLD : (t + 1) * FOLD]
    for n in range(size):
        mix_channels(mix_turned, scratch[n], scratch[size + n])
    low_half = low_lanes(HALF)
    low = low_lanes(B)
    for n in range(size):
        second = scratch[size + n]
        own = own_ref[base + n]
        tiles = []
        for i in range(D // 2):
            pair = own[:, i * FOLD : (i + 1) * FOLD].astype(F32)
            rolled = pltpu.roll(pair, B, 1)
            tiles.append(jnp.where(low_half, pair[:HALF], rolled[HALF:]))
            tiles.append(jnp.where(low_half, rolled[:HALF], pair[HALF:]))
        turned = jnp.concatenate(tiles, axis=0).T.astype(BF)
        for v in range(0, W, 2):
            right = jnp.concatenate([mixed_rows(second, v + i) for i in range(2)], axis=1)
            product = dot(turned, right)
            for i in range(2):
                block = product[:, i * FOLD : (i + 1) * FOLD]
                chosen = jnp.where(low, block[:B], block[B:])
                total = chosen + pltpu.roll(chosen, B, 1)
                folded = jnp.where(low_half, total[:HALF], total[HALF:])
                out_ref[n, (v + i) * HALF : (v + i + 1) * HALF, :] = folded.astype(BF)


def build_environment(half, sectors, slot, local, environment, site, came, mix):
    step = 2
    whole = lambda shape: pl.BlockSpec(shape, lambda l, *refs: (0,) * len(shape))
    return pl.pallas_call(
        functools.partial(build_kernel, half),
        out_shape=jax.ShapeDtypeStruct((sectors, ROWS, FOLD), BF),
        grid_spec=pltpu.PrefetchScalarGridSpec(
            num_scalar_prefetch=2,
            grid=(sectors // step,),
            in_specs=[
                pl.BlockSpec((step, ROWS, FOLD), lambda l, *refs: (l + half // step, 0, 0)),
                whole(site.shape),
                whole(came.shape),
                whole(mix.shape),
            ],
            out_specs=pl.BlockSpec((step, ROWS, FOLD), lambda l, *refs: (l, 0, 0)),
            scratch_shapes=[pltpu.VMEM((MIX * PITCH, FOLD), F32)] * (2 * step),
        ),
        name="build_environment",
        cost_estimate=pl.CostEstimate(flops=10**10, bytes_accessed=10**7, transcendentals=0),
    )(slot, local, environment, site, came, mix)


def gram_sums(gram_ref, entries):
    total = gram_ref[0]
    for g in range(1, gram_ref.shape[0]):
        total = total + gram_ref[g]
    row = total[:1] * (1.0 / entries)
    lane = lax.broadcasted_iota(jnp.int32, (1, FOLD), 1)
    return lambda i: jnp.sum(jnp.where(lane == i, row, 0.0), axis=1, keepdims=True)


def rotation(cross_sum, far, rayleigh_value):
    up, along = -cross_sum, far - rayleigh_value
    scale = jnp.maximum(jnp.abs(up), jnp.abs(along))
    flat = scale == 0.0
    scale = jnp.where(flat, 1.0, scale)
    up, along = up / scale, along / scale
    length = jnp.sqrt(up * up + along * along)
    length = jnp.where(flat, 1.0, length)
    larger = jnp.sqrt(0.5 * (1.0 + jnp.abs(along) / length))
    smaller = jnp.abs(up) / (2.0 * length * larger)
    ahead = along >= 0.0
    cosine = jnp.where(flat, 1.0, jnp.where(ahead, larger, smaller))
    size = jnp.where(ahead, smaller, larger)
    sine = jnp.where(flat, 0.0, jnp.where(cross_sum < 0.0, size, -size))
    return cosine, sine


def correction_scalars(xx, xa, xpa, xpx, papa, papx, pxpx):
    along = xpa - xa * xpx
    square = papa - 2.0 * xa * papx + xa * xa * pxpx
    square = square - 2.0 * along * along + along * along * xx
    return xa, along, lax.rsqrt(jnp.maximum(square, 0.0) + EPSILON)


FIRST = ("uu", "uh", "uPh", "uPu", "PhPh", "PhPu", "PuPu")
LATER = (
    "xx", "xd", "dd", "xa", "xp", "da", "dp", "xPa", "xPp", "dPa", "dPp", "xPx", "xPd", "dPd",
    "PaPa", "PaPp", "PpPp", "PaPx", "PaPd", "PpPx", "PpPd", "PxPx", "PxPd", "PdPd",
)
LAST = ("xa", "xp", "da", "dp")


def split_name(name):
    parts, at = [], 0
    while at < len(name):
        size = 2 if name[at] == "P" else 1
        parts.append(name[at : at + size])
        at += size
    return parts


def first_scalars(gram_ref, entries):
    sums = gram_sums(gram_ref, entries)
    value = {name: sums(i) for i, name in enumerate(FIRST)}
    inverse = lax.rsqrt(value["uu"] + EPSILON)
    square = inverse * inverse
    named = [value[name] * square for name in FIRST]
    return (inverse,) + correction_scalars(*named)


def later_scalars(gram_ref, entries):
    sums = gram_sums(gram_ref, entries)
    value = {name: sums(i) for i, name in enumerate(LATER)}
    cosine, sine = rotation(value["xp"] + value["da"], value["dp"], value["xa"])
    cc, cs, ss = cosine * cosine, cosine * sine, sine * sine

    def turned(a, b, c, d):
        return cc * value[a] + cs * (value[b] + value[c]) + ss * value[d]

    named = (
        turned("xx", "xd", "xd", "dd"),
        turned("xa", "xp", "da", "dp"),
        turned("xPa", "xPp", "dPa", "dPp"),
        turned("xPx", "xPd", "xPd", "dPd"),
        turned("PaPa", "PaPp", "PaPp", "PpPp"),
        turned("PaPx", "PaPd", "PpPx", "PpPd"),
        turned("PxPx", "PxPd", "PxPd", "PdPd"),
    )
    return (cosine, sine) + correction_scalars(*named)


def apply_kernel(mode, entries, *refs):
    flag_ref, slot_ref, local_ref, mix_ref, right_ref, left_ref, early_ref, late_ref = refs[:8]
    refs = refs[8:]
    step_at = pl.program_id(0)
    if mode == "start":
        state_ref, send_ref, own_ref = refs[:3]
        scratch = refs[3:]
    elif mode == "first":
        gram_ref, u_ref, h_ref, weight_ref = refs[:4]
        x_out, a_out, d_out, send_ref, own_ref = refs[4:9]
        scratch = refs[9:]
    else:
        gram_ref, x_ref, a_ref, d_ref, p_ref, weight_ref = refs[:6]
        x_out, a_out, d_out, send_ref, own_ref = refs[6:11]
        scratch = refs[11:]
    fixed, partials = scratch[:2]
    scratch = scratch[2:]
    size = right_ref.shape[0]

    @pl.when(step_at == 0)
    def _():
        own_ref[...] = jnp.zeros_like(own_ref)
        for first in scratch[:size]:
            first[W * D * PITCH :, :] = jnp.zeros(((MIX - W * D) * PITCH, FOLD), F32)
        if mode != "start":
            scalars = first_scalars if mode == "first" else later_scalars
            for i, value in enumerate(scalars(gram_ref, entries)):
                fixed[i : i + 1, :] = jnp.broadcast_to(value, (1, FOLD))

    for n in range(size):
        first = scratch[n]
        if mode == "start":
            vector = state_ref[n]
        else:
            if mode == "first":
                inverse, rho, along, norm = [fixed[i : i + 1, :] for i in range(4)]
                current = inverse * u_ref[n]
                applied = inverse * h_ref[n]
            else:
                cosine, sine, rho, along, norm = [fixed[i : i + 1, :] for i in range(5)]
                current = cosine * x_ref[n] + sine * d_ref[n]
                applied = cosine * a_ref[n] + sine * p_ref[n]
            vector = (weight_ref[n] * (applied - rho * current) - along * current) * norm
            x_out[n] = current
            a_out[n] = applied
            d_out[n] = vector
        right = jnp.concatenate(
            [spread(vector[s * HALF : (s + 1) * HALF]) for s in range(D)], axis=1
        ).astype(BF)
        rows = GROUP * HALF
        for i in range(CLASSES):
            product = dot(right_ref[n, i * rows : (i + 1) * rows, :], right)
            for v in range(GROUP):
                for s in range(D):
                    at = ((i * GROUP + v) * D + s) * PITCH
                    first[at : at + HALF, :] = product[v * HALF : (v + 1) * HALF, s * FOLD : (s + 1) * FOLD]
    for n in range(size):
        mix_channels(mix_ref[...], scratch[n], scratch[size + n])
    own_left = flag_ref[0] == 1
    early = step_at < SEC_DEV // 2 // size
    for n in range(size):
        for k in range(CLASSES):
            rows, blocks = [], []
            for w in range(k * GROUP, (k + 1) * GROUP):
                at = slice(w * HALF, (w + 1) * HALF)
                handed = jnp.where(early, early_ref[n, at, :], late_ref[n, at, :])
                chosen = jnp.where(own_left, left_ref[n, at, :], handed)
                rows.append(mixed_rows(scratch[size + n], w))
                blocks.append(spread(chosen.astype(F32)).astype(BF))
            partial = dot(jnp.concatenate(rows, axis=1), jnp.concatenate(blocks, axis=0))
            partials[n * CLASSES + k] = partial
            send_ref[slot_ref[(step_at * size + n) * CLASSES + k]] = partial.astype(BF)
    for n in range(size):
        for k in range(CLASSES):
            local = local_ref[(step_at * size + n) * CLASSES + k]

            @pl.when(local >= 0)
            def _():
                place = jnp.maximum(local, 0)
                own_ref[place] = own_ref[place] + partials[n * CLASSES + k]


def apply_operator(mode, entries, slots_total, flag, slot, local, mix, right_env, left_envs, gram, vectors):
    step = 2
    halves = SEC_DEV // step // 2
    vector = pl.BlockSpec((step, TILE, FOLD), lambda l, *refs: (l, 0, 0))
    folded = pl.BlockSpec((step, ROWS, FOLD), lambda l, *refs: (l, 0, 0))
    early = pl.BlockSpec((step, ROWS, FOLD), lambda l, *refs: (jnp.minimum(l, halves - 1), 0, 0))
    late = pl.BlockSpec((step, ROWS, FOLD), lambda l, *refs: (jnp.maximum(l - halves, 0), 0, 0))
    whole = lambda shape: pl.BlockSpec(shape, lambda l, *refs: (0,) * len(shape))
    shape = jax.ShapeDtypeStruct((SEC_DEV, TILE, FOLD), F32)
    kept = 0 if mode == "start" else 3
    send = jax.ShapeDtypeStruct((slots_total, TILE, FOLD), BF)
    inputs = (mix, right_env) + tuple(left_envs) + (() if gram is None else (gram,)) + tuple(vectors)
    return pl.pallas_call(
        functools.partial(apply_kernel, mode, entries),
        out_shape=(shape,) * kept + (send, shape),
        grid_spec=pltpu.PrefetchScalarGridSpec(
            num_scalar_prefetch=3,
            grid=(SEC_DEV // step,),
            in_specs=[whole(mix.shape), folded, folded, early, late]
            + ([] if gram is None else [whole(gram.shape)])
            + [vector] * len(vectors),
            out_specs=(vector,) * kept + (whole(send.shape), whole(shape.shape)),
            scratch_shapes=[pltpu.VMEM((8, FOLD), F32), pltpu.VMEM((step * CLASSES, TILE, FOLD), F32)]
            + [pltpu.VMEM((MIX * PITCH, FOLD), F32)] * (2 * step),
        ),
        name="apply_" + mode,
        cost_estimate=pl.CostEstimate(flops=10**10, bytes_accessed=10**7, transcendentals=0),
    )(flag, slot, local, *inputs)


def collect_kernel(names, *refs):
    take_ref, left_ref, right_ref = refs[:3]
    came_ref, own_ref = refs[3:5]
    symbols = sorted({part[-1] for name in names for part in split_name(name)} - {"h", "p"})
    weighted = any("P" in name for name in names)
    vectors = refs[5 : 5 + len(symbols)]
    at = 5 + len(symbols)
    weight_ref = None
    if weighted:
        weight_ref = refs[at]
        at += 1
    out_ref, gram_ref, sums = refs[at:]
    result = "h" if names is FIRST else "p"
    step_at = pl.program_id(0)
    count = own_ref.shape[0]

    @pl.when(step_at == 0)
    def _():
        sums[...] = jnp.zeros_like(sums)

    size = 8
    for n in range(count):
        m = step_at * count + n
        total = own_ref[n]
        for k in range(CLASSES):
            place = take_ref[k * SEC_DEV + m]
            part = came_ref[jnp.maximum(place, 0)].astype(F32)
            total = total + jnp.where(place >= 0, part, 0.0)
        total = live_mask(left_ref[m], [right_ref[m * D + t] for t in range(D)]) * total
        out_ref[n] = total
        totals = [jnp.zeros((size, FOLD), F32) for name in names]
        for i in range(TILE // size):
            rows = slice(i * size, (i + 1) * size)
            value = {symbol: ref[n, rows, :] for symbol, ref in zip(symbols, vectors)}
            value[result] = total[rows]
            if weighted:
                weight = weight_ref[n, rows, :]
                for symbol in list(value):
                    value["P" + symbol] = weight * value[symbol]
            for at, name in enumerate(names):
                one, two = split_name(name)
                totals[at] = totals[at] + value[one] * value[two]
        for at in range(len(names)):
            sums[at] = sums[at] + totals[at]

    @pl.when(step_at == SEC_DEV // count - 1)
    def _():
        lane = lax.broadcasted_iota(jnp.int32, (8, FOLD), 1)
        packed = jnp.zeros((8, FOLD), F32)
        for at in range(len(names)):
            packed = jnp.where(lane == at, jnp.sum(sums[at], keepdims=True), packed)
        for g in range(gram_ref.shape[0]):
            gram_ref[g] = packed


def collect(names, groups, take, left_sizes, right_sizes, came, own, vectors, weight):
    step = 4
    vector = pl.BlockSpec((step, TILE, FOLD), lambda m, *refs: (m, 0, 0))
    whole = lambda shape: pl.BlockSpec(shape, lambda m, *refs: (0,) * len(shape))
    extra = () if weight is None else (weight,)
    gram = jax.ShapeDtypeStruct((groups, 8, FOLD), F32)
    return pl.pallas_call(
        functools.partial(collect_kernel, names),
        out_shape=(jax.ShapeDtypeStruct((SEC_DEV, TILE, FOLD), F32), gram),
        grid_spec=pltpu.PrefetchScalarGridSpec(
            num_scalar_prefetch=3,
            grid=(SEC_DEV // step,),
            in_specs=[whole(came.shape)] + [vector] * (1 + len(vectors) + len(extra)),
            out_specs=(vector, whole(gram.shape)),
            scratch_shapes=[pltpu.VMEM((len(names), 8, FOLD), F32)],
        ),
        name="collect",
        cost_estimate=pl.CostEstimate(flops=10**7, bytes_accessed=4 * 10**6, transcendentals=0),
    )(take, left_sizes, right_sizes, came, own, *vectors, *extra)


def finish_kernel(entries, gram_ref, x_ref, d_ref, state_ref, energy_ref, fixed):
    l = pl.program_id(0)

    @pl.when(l == 0)
    def _():
        sums = gram_sums(gram_ref, entries)
        xa, xp, da, dp = [sums(i) for i in range(4)]
        cosine, sine = rotation(xp + da, dp, xa)
        energy = cosine * cosine * xa + cosine * sine * (xp + da) + sine * sine * dp
        fixed[0:1, :] = jnp.broadcast_to(cosine, (1, FOLD))
        fixed[1:2, :] = jnp.broadcast_to(sine, (1, FOLD))
        energy_ref[...] = jnp.broadcast_to(energy, energy_ref.shape)

    for n in range(x_ref.shape[0]):
        final = fixed[0:1, :] * x_ref[n] + fixed[1:2, :] * d_ref[n]
        for i in range(D // 2):
            first = final[(2 * i) * HALF : (2 * i + 1) * HALF]
            second = final[(2 * i + 1) * HALF : (2 * i + 2) * HALF]
            state_ref[n, :, i * FOLD : (i + 1) * FOLD] = unfold_pair(first, second)


def finish(entries, gram, current, direction):
    step = 4
    vector = pl.BlockSpec((step, TILE, FOLD), lambda l: (l, 0, 0))
    return pl.pallas_call(
        functools.partial(finish_kernel, entries),
        grid=(SEC_DEV // step,),
        out_shape=(
            jax.ShapeDtypeStruct((SEC_DEV, B, D * B), F32),
            jax.ShapeDtypeStruct((8, FOLD), F32),
        ),
        in_specs=[pl.BlockSpec(gram.shape, lambda l: (0, 0, 0)), vector, vector],
        out_specs=(
            pl.BlockSpec((step, B, D * B), lambda l: (l, 0, 0)),
            pl.BlockSpec((8, FOLD), lambda l: (0, 0)),
        ),
        scratch_shapes=[pltpu.VMEM((8, FOLD), F32)],
        name="finish",
        cost_estimate=pl.CostEstimate(flops=10**6, bytes_accessed=2 * 10**6, transcendentals=0),
    )(gram, current, direction)


def exchange(blocks):
    return lax.all_to_all(blocks, "sec", 0, 0, tiled=True)


def on_device(
    left_environment,
    right_environment,
    site_previous,
    state_start,
    preconditioner,
    channel_tensor,
    channel_mask,
    sector_shift,
    left_sizes,
    right_sizes,
):
    groups = lax.axis_size("sec")
    my_group = lax.axis_index("sec")
    offset = my_group * SEC_DEV
    slots = (PAIRS + groups - 1) // groups
    entries = float(SEC_DEV * B * D * B * groups)
    my_left = lax.dynamic_slice_in_dim(left_sizes, offset, SEC_DEV, 0)
    my_right = lax.dynamic_slice_in_dim(right_sizes, offset, SEC_DEV, 0).reshape(SEC_DEV * D)
    position = lax.axis_index("seg")
    last = lax.axis_size("seg") - 1

    at_end = (position == last).astype(jnp.int32)[None]
    at_start = (position == 0).astype(jnp.int32)[None]
    came_right = passed_along(right_environment[0], "seg", -1)

    slot, local, take, site_send = route(my_group[None], sector_shift, site_previous[0], groups, slots)
    site_came = exchange(site_send).reshape(groups * slots, B, D * B)
    mix = channel_tensor * channel_mask.astype(BF)[:, None, :, None]
    mix = jnp.pad(mix.reshape(W * D, W * D), ((0, MIX - W * D), (0, MIX - W * D)))

    own_left = fold_environment(at_start, left_environment[0])
    handed = []
    for half in range(2):
        sectors = SEC_DEV // 2
        fresh = build_environment(
            half * sectors, sectors, slot, local, own_left, site_previous[0], site_came, mix
        )
        handed.append(passed_along(fresh, "seg", 1))
    right_env = fold_environment(at_end, right_environment[0], came_right)
    start, weight = fold_state(my_left, my_right, state_start[0], preconditioner[0])

    apply = functools.partial(
        apply_operator, entries=entries, slots_total=groups * slots, flag=at_start, slot=slot, local=local,
        mix=mix, right_env=right_env, left_envs=(own_left, *handed),
    )

    def gather(names, send, own, vectors, weight):
        came = exchange(send.reshape(groups, slots, TILE, FOLD)).reshape(groups * slots, TILE, FOLD)
        result, gram = collect(names, groups, take, my_left, my_right, came, own, vectors, weight)
        return result, exchange(gram)

    send, own = apply("start", gram=None, vectors=(start,))
    product, gram = gather(FIRST, send, own, (start,), weight)
    current, applied, direction, send, own = apply("first", gram=gram, vectors=(start, product, weight))
    product, gram = gather(LATER, send, own, (applied, direction, current), weight)
    current, applied, direction, send, own = apply(
        "later", gram=gram, vectors=(current, applied, direction, product, weight)
    )
    product, gram = gather(LAST, send, own, (applied, direction, current), None)
    state, energy = finish(entries, gram, current, direction)
    return (state[None], energy[0, :1])


def solution(mesh):
    in_specs = (
        P("seg", "sec", None, None),
        P("seg", "sec", None, None),
        P("seg", "sec", None, None),
        P("seg", "sec", None, None),
        P("seg", "sec", None, None),
        P(),
        P(),
        P(),
        P(),
        P(),
    )
    out_specs = (P("seg", "sec", None, None), P("seg"))
    return jax.shard_map(
        on_device, mesh=mesh, in_specs=in_specs, out_specs=out_specs, check_vma=False
    )
```

```python
import functools

import jax
import jax.numpy as jnp
from jax import lax
from jax.experimental import pallas as pl
from jax.experimental.pallas import tpu as pltpu
from jax.sharding import PartitionSpec as P

W = 30
D = 4
B = 64
SEC_DEV = 8
CLASSES = 5
GROUP = W // CLASSES
PAIRS = SEC_DEV * CLASSES
SHIFT = SEC_DEV.bit_length() - 1
HALF = B // 2
FOLD = 2 * B
ROWS = W * HALF
TILE = D * HALF
MIX = 128
PITCH = 33
EPSILON = 1e-06
BF = jnp.bfloat16
F32 = jnp.float32


def passed_along(block, axis, distance):
    devices = range(lax.axis_size(axis))
    route = [(i - distance, i) for i in devices if i - distance in devices]
    return lax.ppermute(block, axis, route)


def low_lanes(rows):
    return lax.broadcasted_iota(jnp.int32, (rows, FOLD), 1) < B


def fold_pair(pair):
    stacked = jnp.concatenate([pair, pltpu.roll(pair, FOLD - HALF, 1)], axis=0)
    turned = stacked.T
    return turned[:HALF], turned[B : B + HALF]


def unfold_pair(first, second):
    filler = jnp.zeros((HALF, FOLD), F32)
    turned = jnp.concatenate([first, filler, second, filler], axis=0).T
    upper = lax.broadcasted_iota(jnp.int32, (B, FOLD), 1) % B < HALF
    return jnp.where(upper, turned[:B], pltpu.roll(turned[B:], HALF, 1))


def spread(tile):
    rolled = pltpu.roll(tile, B, 1)
    low = low_lanes(HALF)
    zero = jnp.zeros_like(tile)
    return jnp.concatenate(
        [
            jnp.where(low, tile, zero),
            jnp.where(low, rolled, zero),
            jnp.where(low, zero, rolled),
            jnp.where(low, zero, tile),
        ],
        axis=0,
    )


def spread_pair(pair):
    rolled = pltpu.roll(pair, B, 1)
    low = low_lanes(B)
    zero = jnp.zeros_like(pair)
    first = jnp.concatenate([jnp.where(low, pair, zero), jnp.where(low, zero, rolled)], axis=0)
    second = jnp.concatenate([jnp.where(low, rolled, zero), jnp.where(low, zero, pair)], axis=0)
    return first, second


def dot(left, right):
    return jnp.dot(left, right, preferred_element_type=F32)


def route_kernel(me_ref, shift_ref, source_ref, site_ref, slot_ref, local_ref, take_ref, send_ref, count, source):
    groups = send_ref.shape[0]
    slots = send_ref.shape[1]
    me = me_ref[0]
    for g in range(groups):
        count[g] = 0
        count[groups + g] = 0
    for i in range(groups * slots):
        source[i] = 0
    for k in range(CLASSES):
        targets = [shift_ref[k, me * SEC_DEV + l] for l in range(SEC_DEV)]
        owners = [target >> SHIFT for target in targets]
        ranks = [count[owner] for owner in owners]
        for one in range(SEC_DEV):
            for two in range(one):
                same = owners[one] == owners[two]
                above = targets[one] > targets[two]
                ranks[one] = ranks[one] + (same & above).astype(jnp.int32)
                ranks[two] = ranks[two] + (same & jnp.logical_not(above)).astype(jnp.int32)
        for l in range(SEC_DEV):
            slot_ref[l * CLASSES + k] = owners[l] * slots + jnp.minimum(ranks[l], slots - 1)
            local_ref[l * CLASSES + k] = jnp.where(owners[l] == me, targets[l] & (SEC_DEV - 1), -1)
        for owner in owners:
            count[owner] = count[owner] + 1
        for m in range(SEC_DEV):
            g = source_ref[k, m] >> SHIFT
            rank = count[groups + g]
            count[groups + g] = rank + 1
            place = g * slots + jnp.minimum(rank, slots - 1)
            take_ref[k * SEC_DEV + m] = jnp.where(g == me, -1, place)
            source[place] = m

    def one_copy(g, carry):
        for r in range(slots):
            send_ref[g, r] = site_ref[source[g * slots + r]]
        return carry

    lax.fori_loop(0, groups, one_copy, 0)


def route(me, sector_shift, site, groups, slots):
    mine = me * SEC_DEV + jnp.arange(SEC_DEV, dtype=jnp.int32)
    sector = jnp.arange(sector_shift.shape[1], dtype=jnp.int32)
    hit = sector_shift[:, None, :] == mine[None, :, None]
    source = jnp.sum(jnp.where(hit, sector[None, None, :], 0), axis=2)
    smem = pl.BlockSpec(memory_space=pltpu.SMEM)
    vmem = pl.BlockSpec(memory_space=pltpu.VMEM)
    return pl.pallas_call(
        route_kernel,
        out_shape=(
            jax.ShapeDtypeStruct((PAIRS,), jnp.int32),
            jax.ShapeDtypeStruct((PAIRS,), jnp.int32),
            jax.ShapeDtypeStruct((PAIRS,), jnp.int32),
            jax.ShapeDtypeStruct((groups, slots, B, D * B), BF),
        ),
        in_specs=[smem, smem, smem, vmem],
        out_specs=(smem, smem, smem, vmem),
        scratch_shapes=[
            pltpu.SMEM((2 * groups,), jnp.int32),
            pltpu.SMEM((groups * slots,), jnp.int32),
        ],
        name="route",
    )(me[None], sector_shift, source, site)


def fold_environment_kernel(flag_ref, *refs):
    out_ref = refs[-1]
    for n in range(out_ref.shape[0]):
        for i in range(W // 2):
            pairs = [ref[n, :, i * FOLD : (i + 1) * FOLD].astype(F32) for ref in refs[:-1]]
            pair = pairs[0] if len(pairs) == 1 else jnp.where(flag_ref[0] == 1, pairs[0], pairs[1])
            first, second = fold_pair(pair)
            out_ref[n, (2 * i) * HALF : (2 * i + 1) * HALF, :] = first.astype(BF)
            out_ref[n, (2 * i + 1) * HALF : (2 * i + 2) * HALF, :] = second.astype(BF)


def fold_environment(flag, *environments):
    step = 2
    return pl.pallas_call(
        fold_environment_kernel,
        out_shape=jax.ShapeDtypeStruct((SEC_DEV, ROWS, FOLD), BF),
        grid_spec=pltpu.PrefetchScalarGridSpec(
            num_scalar_prefetch=1,
            grid=(SEC_DEV // step,),
            in_specs=[pl.BlockSpec((step, B, W * B), lambda l, *refs: (l, 0, 0))] * len(environments),
            out_specs=pl.BlockSpec((step, ROWS, FOLD), lambda l, *refs: (l, 0, 0)),
        ),
        name="fold_environment",
        cost_estimate=pl.CostEstimate(
            flops=0, bytes_accessed=4 * SEC_DEV * ROWS * FOLD, transcendentals=0
        ),
    )(flag, *environments)


def live_mask(left_size, right_sizes):
    half_p = lax.broadcasted_iota(jnp.int32, (HALF, FOLD), 1)
    column = lax.broadcasted_iota(jnp.int32, (HALF, FOLD), 0) + jnp.where(half_p < B, 0, HALF)
    row = jnp.where(half_p < B, half_p, half_p - B)
    parts = [
        jnp.where((row < left_size) & (column < right_sizes[t]), 1.0, 0.0).astype(F32) for t in range(D)
    ]
    return jnp.concatenate(parts, axis=0)


def fold_state_kernel(left_ref, right_ref, state_ref, weight_ref, start_ref, fold_ref):
    for n in range(state_ref.shape[0]):
        l = pl.program_id(0) * state_ref.shape[0] + n
        mask = live_mask(left_ref[l], [right_ref[l * D + t] for t in range(D)])
        for source, result in ((state_ref, start_ref), (weight_ref, fold_ref)):
            tiles = []
            for i in range(D // 2):
                tiles.extend(fold_pair(source[n, :, i * FOLD : (i + 1) * FOLD]))
            folded = jnp.concatenate(tiles, axis=0)
            result[n] = mask * folded if result is start_ref else folded


def fold_state(left_sizes, right_sizes, state, weight):
    step = 4
    natural = pl.BlockSpec((step, B, D * B), lambda l, *refs: (l, 0, 0))
    folded = pl.BlockSpec((step, TILE, FOLD), lambda l, *refs: (l, 0, 0))
    shape = jax.ShapeDtypeStruct((SEC_DEV, TILE, FOLD), F32)
    return pl.pallas_call(
        fold_state_kernel,
        out_shape=(shape, shape),
        grid_spec=pltpu.PrefetchScalarGridSpec(
            num_scalar_prefetch=2,
            grid=(SEC_DEV // step,),
            in_specs=[natural, natural],
            out_specs=(folded, folded),
        ),
        name="fold_state",
        cost_estimate=pl.CostEstimate(flops=0, bytes_accessed=16 * SEC_DEV * TILE * FOLD, transcendentals=0),
    )(left_sizes, right_sizes, state, weight)


def mix_channels(mix, first, second):
    for j in range(0, HALF, 2):
        parts = [first[pl.ds(j + i, MIX, stride=PITCH), :].astype(BF) for i in range(2)]
        mixed = dot(mix, jnp.concatenate(parts, axis=1))
        for i in range(2):
            second[pl.ds(j + i, MIX, stride=PITCH), :] = mixed[:, i * FOLD : (i + 1) * FOLD]


def mixed_rows(ref, x):
    return jnp.concatenate(
        [ref[(x * D + y) * PITCH : (x * D + y) * PITCH + HALF, :].astype(BF) for y in range(D)], axis=0
    )


def build_kernel(half, slot_ref, local_ref, env_ref, own_ref, came_ref, mix_ref, out_ref, *scratch):
    size = env_ref.shape[0]
    base = half + pl.program_id(0) * size

    @pl.when(pl.program_id(0) == 0)
    def _():
        for first in scratch[:size]:
            first[W * D * PITCH :, :] = jnp.zeros(((MIX - W * D) * PITCH, FOLD), F32)

    mix_turned = mix_ref[...].astype(F32).T.astype(BF)
    for n in range(size):
        first = scratch[n]
        for k in range(CLASSES):
            slot = slot_ref[(base + n) * CLASSES + k]
            local = local_ref[(base + n) * CLASSES + k]
            tensor = jnp.where(local >= 0, own_ref[jnp.maximum(local, 0)], came_ref[slot])
            blocks = []
            for i in range(D // 2):
                blocks.extend(spread_pair(tensor[:, i * FOLD : (i + 1) * FOLD].astype(F32)))
            right = jnp.concatenate(blocks, axis=1).astype(BF)
            left = env_ref[n, k * GROUP * HALF : (k + 1) * GROUP * HALF, :]
            joined = dot(left, right)
            for j in range(GROUP):
                for t in range(D):
                    at = ((k * GROUP + j) * D + t) * PITCH
                    first[at : at + HALF, :] = joined[j * HALF : (j + 1) * HALF, t * FOLD : (t + 1) * FOLD]
    for n in range(size):
        mix_channels(mix_turned, scratch[n], scratch[size + n])
    low_half = low_lanes(HALF)
    low = low_lanes(B)
    for n in range(size):
        second = scratch[size + n]
        own = own_ref[base + n]
        tiles = []
        for i in range(D // 2):
            pair = own[:, i * FOLD : (i + 1) * FOLD].astype(F32)
            rolled = pltpu.roll(pair, B, 1)
            tiles.append(jnp.where(low_half, pair[:HALF], rolled[HALF:]))
            tiles.append(jnp.where(low_half, rolled[:HALF], pair[HALF:]))
        turned = jnp.concatenate(tiles, axis=0).T.astype(BF)
        for v in range(0, W, 2):
            right = jnp.concatenate([mixed_rows(second, v + i) for i in range(2)], axis=1)
            product = dot(turned, right)
            for i in range(2):
                block = product[:, i * FOLD : (i + 1) * FOLD]
                chosen = jnp.where(low, block[:B], block[B:])
                total = chosen + pltpu.roll(chosen, B, 1)
                folded = jnp.where(low_half, total[:HALF], total[HALF:])
                out_ref[n, (v + i) * HALF : (v + i + 1) * HALF, :] = folded.astype(BF)


def build_environment(half, sectors, slot, local, environment, site, came, mix):
    step = 2
    whole = lambda shape: pl.BlockSpec(shape, lambda l, *refs: (0,) * len(shape))
    return pl.pallas_call(
        functools.partial(build_kernel, half),
        out_shape=jax.ShapeDtypeStruct((sectors, ROWS, FOLD), BF),
        grid_spec=pltpu.PrefetchScalarGridSpec(
            num_scalar_prefetch=2,
            grid=(sectors // step,),
            in_specs=[
                pl.BlockSpec((step, ROWS, FOLD), lambda l, *refs: (l + half // step, 0, 0)),
                whole(site.shape),
                whole(came.shape),
                whole(mix.shape),
            ],
            out_specs=pl.BlockSpec((step, ROWS, FOLD), lambda l, *refs: (l, 0, 0)),
            scratch_shapes=[pltpu.VMEM((MIX * PITCH, FOLD), F32)] * (2 * step),
        ),
        name="build_environment",
        cost_estimate=pl.CostEstimate(flops=10**10, bytes_accessed=10**7, transcendentals=0),
    )(slot, local, environment, site, came, mix)


def gram_sums(gram_ref, entries):
    total = gram_ref[0]
    for g in range(1, gram_ref.shape[0]):
        total = total + gram_ref[g]
    row = total[:1] * (1.0 / entries)
    lane = lax.broadcasted_iota(jnp.int32, (1, FOLD), 1)
    return lambda i: jnp.sum(jnp.where(lane == i, row, 0.0), axis=1, keepdims=True)


def rotation(cross_sum, far, rayleigh_value):
    up, along = -cross_sum, far - rayleigh_value
    scale = jnp.maximum(jnp.abs(up), jnp.abs(along))
    flat = scale == 0.0
    scale = jnp.where(flat, 1.0, scale)
    up, along = up / scale, along / scale
    length = jnp.sqrt(up * up + along * along)
    length = jnp.where(flat, 1.0, length)
    larger = jnp.sqrt(0.5 * (1.0 + jnp.abs(along) / length))
    smaller = jnp.abs(up) / (2.0 * length * larger)
    ahead = along >= 0.0
    cosine = jnp.where(flat, 1.0, jnp.where(ahead, larger, smaller))
    size = jnp.where(ahead, smaller, larger)
    sine = jnp.where(flat, 0.0, jnp.where(cross_sum < 0.0, size, -size))
    return cosine, sine


def correction_scalars(xx, xa, xpa, xpx, papa, papx, pxpx):
    along = xpa - xa * xpx
    square = papa - 2.0 * xa * papx + xa * xa * pxpx
    square = square - 2.0 * along * along + along * along * xx
    return xa, along, lax.rsqrt(jnp.maximum(square, 0.0) + EPSILON)


FIRST = ("uu", "uh", "uPh", "uPu", "PhPh", "PhPu", "PuPu")
LATER = (
    "xx", "xd", "dd", "xa", "xp", "da", "dp", "xPa", "xPp", "dPa", "dPp", "xPx", "xPd", "dPd",
    "PaPa", "PaPp", "PpPp", "PaPx", "PaPd", "PpPx", "PpPd", "PxPx", "PxPd", "PdPd",
)
LAST = ("xa", "xp", "da", "dp")


def split_name(name):
    parts, at = [], 0
    while at < len(name):
        size = 2 if name[at] == "P" else 1
        parts.append(name[at : at + size])
        at += size
    return parts


def first_scalars(gram_ref, entries):
    sums = gram_sums(gram_ref, entries)
    value = {name: sums(i) for i, name in enumerate(FIRST)}
    inverse = lax.rsqrt(value["uu"] + EPSILON)
    square = inverse * inverse
    named = [value[name] * square for name in FIRST]
    return (inverse,) + correction_scalars(*named)


def later_scalars(gram_ref, entries):
    sums = gram_sums(gram_ref, entries)
    value = {name: sums(i) for i, name in enumerate(LATER)}
    cosine, sine = rotation(value["xp"] + value["da"], value["dp"], value["xa"])
    cc, cs, ss = cosine * cosine, cosine * sine, sine * sine

    def turned(a, b, c, d):
        return cc * value[a] + cs * (value[b] + value[c]) + ss * value[d]

    named = (
        turned("xx", "xd", "xd", "dd"),
        turned("xa", "xp", "da", "dp"),
        turned("xPa", "xPp", "dPa", "dPp"),
        turned("xPx", "xPd", "xPd", "dPd"),
        turned("PaPa", "PaPp", "PaPp", "PpPp"),
        turned("PaPx", "PaPd", "PpPx", "PpPd"),
        turned("PxPx", "PxPd", "PxPd", "PdPd"),
    )
    return (cosine, sine) + correction_scalars(*named)


def clear_padding(scratch):
    for first in scratch:
        first[W * D * PITCH :, :] = jnp.zeros(((MIX - W * D) * PITCH, FOLD), F32)


def contract_right(vector, right_ref, n, first):
    right = jnp.concatenate([spread(vector[s * HALF : (s + 1) * HALF]) for s in range(D)], axis=1).astype(BF)
    rows = GROUP * HALF
    for i in range(CLASSES):
        product = dot(right_ref[n, i * rows : (i + 1) * rows, :], right)
        for v in range(GROUP):
            for s in range(D):
                at = ((i * GROUP + v) * D + s) * PITCH
                first[at : at + HALF, :] = product[v * HALF : (v + 1) * HALF, s * FOLD : (s + 1) * FOLD]


def contract_left(n, own_left, early, left_refs, rows_of, at, slot_ref, send_ref, partials):
    left_ref, early_ref, late_ref = left_refs
    for k in range(CLASSES):
        rows, blocks = [], []
        for w in range(k * GROUP, (k + 1) * GROUP):
            part = slice(w * HALF, (w + 1) * HALF)
            handed = jnp.where(early, early_ref[n, part, :], late_ref[n, part, :])
            chosen = jnp.where(own_left, left_ref[n, part, :], handed)
            rows.append(rows_of(w))
            blocks.append(spread(chosen.astype(F32)).astype(BF))
        partial = dot(jnp.concatenate(rows, axis=1), jnp.concatenate(blocks, axis=0))
        partials[n * CLASSES + k] = partial
        send_ref[slot_ref[at * CLASSES + k]] = partial.astype(BF)


def add_own(base, size, local_ref, own_ref, partials):
    for n in range(size):
        for k in range(CLASSES):
            local = local_ref[(base + n) * CLASSES + k]

            @pl.when(local >= 0)
            def _():
                place = jnp.maximum(local, 0)
                own_ref[place] = own_ref[place] + partials[n * CLASSES + k]


def mix_start_kernel(mix_ref, right_ref, state_ref, out_ref, *scratch):
    size = right_ref.shape[0]

    @pl.when(pl.program_id(0) == 0)
    def _():
        clear_padding(scratch[:size])

    for n in range(size):
        contract_right(state_ref[n], right_ref, n, scratch[n])
    for n in range(size):
        mix_channels(mix_ref[...], scratch[n], scratch[size + n])
    for n in range(size):
        for w in range(W):
            out_ref[n, w * TILE : (w + 1) * TILE, :] = mixed_rows(scratch[size + n], w)


def mix_start(mix, right_env, start):
    step = 2
    block = lambda rows: pl.BlockSpec((step, rows, FOLD), lambda l: (l, 0, 0))
    return pl.pallas_call(
        mix_start_kernel,
        grid=(SEC_DEV // step,),
        out_shape=jax.ShapeDtypeStruct((SEC_DEV, W * TILE, FOLD), BF),
        in_specs=[pl.BlockSpec(mix.shape, lambda l: (0, 0)), block(ROWS), block(TILE)],
        out_specs=block(W * TILE),
        scratch_shapes=[pltpu.VMEM((MIX * PITCH, FOLD), F32)] * (2 * step),
        name="mix_start",
        cost_estimate=pl.CostEstimate(flops=10**10, bytes_accessed=10**7, transcendentals=0),
    )(mix, right_env, start)


def join_start_kernel(flag_ref, slot_ref, local_ref, mixed_ref, *refs):
    left_refs, (send_ref, own_ref, partials) = refs[:3], refs[3:]
    size = mixed_ref.shape[0]
    base = pl.program_id(0) * size

    @pl.when(base == 0)
    def _():
        own_ref[...] = jnp.zeros_like(own_ref)

    own_left = flag_ref[0] == 1
    early = base < SEC_DEV // 2
    for n in range(size):
        rows_of = lambda w: mixed_ref[n, w * TILE : (w + 1) * TILE, :]
        contract_left(n, own_left, early, left_refs, rows_of, base + n, slot_ref, send_ref, partials)
    add_own(base, size, local_ref, own_ref, partials)


def apply_kernel(mode, entries, *refs):
    flag_ref, slot_ref, local_ref, mix_ref, right_ref = refs[:5]
    left_refs = refs[5:8]
    inputs = refs[8 : 12 if mode == "first" else 14]
    x_out, a_out, d_out, send_ref, own_ref, fixed, partials = refs[8 + len(inputs) : 15 + len(inputs)]
    scratch = refs[15 + len(inputs) :]
    size = right_ref.shape[0]
    base = pl.program_id(0) * size

    @pl.when(base == 0)
    def _():
        own_ref[...] = jnp.zeros_like(own_ref)
        clear_padding(scratch[:size])
        scalars = first_scalars if mode == "first" else later_scalars
        for i, value in enumerate(scalars(inputs[0], entries)):
            fixed[i : i + 1, :] = jnp.broadcast_to(value, (1, FOLD))

    for n in range(size):
        if mode == "first":
            u_ref, h_ref, weight_ref = inputs[1:]
            inverse, rho, along, norm = [fixed[i : i + 1, :] for i in range(4)]
            current = inverse * u_ref[n]
            applied = inverse * h_ref[n]
        else:
            x_ref, a_ref, d_ref, p_ref, weight_ref = inputs[1:]
            cosine, sine, rho, along, norm = [fixed[i : i + 1, :] for i in range(5)]
            current = cosine * x_ref[n] + sine * d_ref[n]
            applied = cosine * a_ref[n] + sine * p_ref[n]
        vector = (weight_ref[n] * (applied - rho * current) - along * current) * norm
        x_out[n] = current
        a_out[n] = applied
        d_out[n] = vector
        contract_right(vector, right_ref, n, scratch[n])
    for n in range(size):
        mix_channels(mix_ref[...], scratch[n], scratch[size + n])
    own_left = flag_ref[0] == 1
    early = base < SEC_DEV // 2
    for n in range(size):
        rows_of = functools.partial(mixed_rows, scratch[size + n])
        contract_left(n, own_left, early, left_refs, rows_of, base + n, slot_ref, send_ref, partials)
    add_own(base, size, local_ref, own_ref, partials)


def apply_operator(mode, entries, slots_total, tables, left_envs, fixed_inputs, vectors):
    step = 2
    halves = SEC_DEV // step // 2
    vector = pl.BlockSpec((step, TILE, FOLD), lambda l, *refs: (l, 0, 0))
    folded = pl.BlockSpec((step, ROWS, FOLD), lambda l, *refs: (l, 0, 0))
    early = pl.BlockSpec((step, ROWS, FOLD), lambda l, *refs: (jnp.minimum(l, halves - 1), 0, 0))
    late = pl.BlockSpec((step, ROWS, FOLD), lambda l, *refs: (jnp.maximum(l - halves, 0), 0, 0))
    whole = lambda shape: pl.BlockSpec(shape, lambda l, *refs: (0,) * len(shape))
    shape = jax.ShapeDtypeStruct((SEC_DEV, TILE, FOLD), F32)
    send = jax.ShapeDtypeStruct((slots_total, TILE, FOLD), BF)
    lefts = [folded, early, late]
    partials = [pltpu.VMEM((step * CLASSES, TILE, FOLD), F32)]
    if mode == "start":
        kernel, kept = join_start_kernel, 0
        (mixed,) = fixed_inputs
        inputs = (mixed, *left_envs)
        in_specs = [pl.BlockSpec((step, W * TILE, FOLD), lambda l, *refs: (l, 0, 0))] + lefts
        scratch = partials
    else:
        kernel, kept = functools.partial(apply_kernel, mode, entries), 3
        mix, right_env, gram = fixed_inputs
        inputs = (mix, right_env, *left_envs, gram, *vectors)
        in_specs = [whole(mix.shape), folded] + lefts + [whole(gram.shape)] + [vector] * len(vectors)
        scratch = [pltpu.VMEM((8, FOLD), F32)] + partials
        scratch += [pltpu.VMEM((MIX * PITCH, FOLD), F32)] * (2 * step)
    return pl.pallas_call(
        kernel,
        out_shape=(shape,) * kept + (send, shape),
        grid_spec=pltpu.PrefetchScalarGridSpec(
            num_scalar_prefetch=3,
            grid=(SEC_DEV // step,),
            in_specs=in_specs,
            out_specs=(vector,) * kept + (whole(send.shape), whole(shape.shape)),
            scratch_shapes=scratch,
        ),
        cost_estimate=pl.CostEstimate(flops=10**10, bytes_accessed=10**7, transcendentals=0),
    )(*tables, *inputs)


def collect_kernel(names, *refs):
    take_ref, left_ref, right_ref = refs[:3]
    came_ref, own_ref = refs[3:5]
    symbols = sorted({part[-1] for name in names for part in split_name(name)} - {"h", "p"})
    weighted = any("P" in name for name in names)
    vectors = refs[5 : 5 + len(symbols)]
    at = 5 + len(symbols)
    weight_ref = None
    if weighted:
        weight_ref = refs[at]
        at += 1
    out_ref, gram_ref, sums = refs[at:]
    result = "h" if names is FIRST else "p"
    step_at = pl.program_id(0)
    count = own_ref.shape[0]

    @pl.when(step_at == 0)
    def _():
        sums[...] = jnp.zeros_like(sums)

    size = 8
    for n in range(count):
        m = step_at * count + n
        total = own_ref[n]
        for k in range(CLASSES):
            place = take_ref[k * SEC_DEV + m]
            part = came_ref[jnp.maximum(place, 0)].astype(F32)
            total = total + jnp.where(place >= 0, part, 0.0)
        total = live_mask(left_ref[m], [right_ref[m * D + t] for t in range(D)]) * total
        out_ref[n] = total
        totals = [jnp.zeros((size, FOLD), F32) for name in names]
        for i in range(TILE // size):
            rows = slice(i * size, (i + 1) * size)
            value = {symbol: ref[n, rows, :] for symbol, ref in zip(symbols, vectors)}
            value[result] = total[rows]
            if weighted:
                weight = weight_ref[n, rows, :]
                for symbol in list(value):
                    value["P" + symbol] = weight * value[symbol]
            for at, name in enumerate(names):
                one, two = split_name(name)
                totals[at] = totals[at] + value[one] * value[two]
        for at in range(len(names)):
            sums[at] = sums[at] + totals[at]

    @pl.when(step_at == SEC_DEV // count - 1)
    def _():
        lane = lax.broadcasted_iota(jnp.int32, (8, FOLD), 1)
        packed = jnp.zeros((8, FOLD), F32)
        for at in range(len(names)):
            packed = jnp.where(lane == at, jnp.sum(sums[at], keepdims=True), packed)
        for g in range(gram_ref.shape[0]):
            gram_ref[g] = packed


def collect(names, groups, take, left_sizes, right_sizes, came, own, vectors, weight):
    step = 4
    vector = pl.BlockSpec((step, TILE, FOLD), lambda m, *refs: (m, 0, 0))
    whole = lambda shape: pl.BlockSpec(shape, lambda m, *refs: (0,) * len(shape))
    extra = () if weight is None else (weight,)
    gram = jax.ShapeDtypeStruct((groups, 8, FOLD), F32)
    return pl.pallas_call(
        functools.partial(collect_kernel, names),
        out_shape=(jax.ShapeDtypeStruct((SEC_DEV, TILE, FOLD), F32), gram),
        grid_spec=pltpu.PrefetchScalarGridSpec(
            num_scalar_prefetch=3,
            grid=(SEC_DEV // step,),
            in_specs=[whole(came.shape)] + [vector] * (1 + len(vectors) + len(extra)),
            out_specs=(vector, whole(gram.shape)),
            scratch_shapes=[pltpu.VMEM((len(names), 8, FOLD), F32)],
        ),
        name="collect",
        cost_estimate=pl.CostEstimate(flops=10**7, bytes_accessed=4 * 10**6, transcendentals=0),
    )(take, left_sizes, right_sizes, came, own, *vectors, *extra)


def finish_kernel(entries, gram_ref, x_ref, d_ref, state_ref, energy_ref, fixed):
    l = pl.program_id(0)

    @pl.when(l == 0)
    def _():
        sums = gram_sums(gram_ref, entries)
        xa, xp, da, dp = [sums(i) for i in range(4)]
        cosine, sine = rotation(xp + da, dp, xa)
        energy = cosine * cosine * xa + cosine * sine * (xp + da) + sine * sine * dp
        fixed[0:1, :] = jnp.broadcast_to(cosine, (1, FOLD))
        fixed[1:2, :] = jnp.broadcast_to(sine, (1, FOLD))
        energy_ref[0] = jnp.sum(energy)

    for n in range(x_ref.shape[0]):
        final = fixed[0:1, :] * x_ref[n] + fixed[1:2, :] * d_ref[n]
        for i in range(D // 2):
            first = final[(2 * i) * HALF : (2 * i + 1) * HALF]
            second = final[(2 * i + 1) * HALF : (2 * i + 2) * HALF]
            state_ref[n, :, i * FOLD : (i + 1) * FOLD] = unfold_pair(first, second)


def finish(entries, gram, current, direction):
    step = 4
    vector = pl.BlockSpec((step, TILE, FOLD), lambda l: (l, 0, 0))
    return pl.pallas_call(
        functools.partial(finish_kernel, entries),
        grid=(SEC_DEV // step,),
        out_shape=(
            jax.ShapeDtypeStruct((SEC_DEV, B, D * B), F32),
            jax.ShapeDtypeStruct((1,), F32),
        ),
        in_specs=[pl.BlockSpec(gram.shape, lambda l: (0, 0, 0)), vector, vector],
        out_specs=(
            pl.BlockSpec((step, B, D * B), lambda l: (l, 0, 0)),
            pl.BlockSpec(memory_space=pltpu.SMEM),
        ),
        scratch_shapes=[pltpu.VMEM((8, FOLD), F32)],
        name="finish",
        cost_estimate=pl.CostEstimate(flops=10**6, bytes_accessed=2 * 10**6, transcendentals=0),
    )(gram, current, direction)


def exchange(blocks):
    return lax.all_to_all(blocks, "sec", 0, 0, tiled=True)


def on_device(
    left_environment,
    right_environment,
    site_previous,
    state_start,
    preconditioner,
    channel_tensor,
    channel_mask,
    sector_shift,
    left_sizes,
    right_sizes,
):
    groups = lax.axis_size("sec")
    my_group = lax.axis_index("sec")
    offset = my_group * SEC_DEV
    slots = (PAIRS + groups - 1) // groups
    entries = float(SEC_DEV * B * D * B * groups)
    my_left = lax.dynamic_slice_in_dim(left_sizes, offset, SEC_DEV, 0)
    my_right = lax.dynamic_slice_in_dim(right_sizes, offset, SEC_DEV, 0).reshape(SEC_DEV * D)
    position = lax.axis_index("seg")
    last = lax.axis_size("seg") - 1

    at_end = (position == last).astype(jnp.int32)[None]
    at_start = (position == 0).astype(jnp.int32)[None]
    came_right = passed_along(right_environment[0], "seg", -1)
    slot, local, take, site_send = route(my_group, sector_shift, site_previous[0], groups, slots)
    site_came = exchange(site_send).reshape(groups * slots, B, D * B)
    mix = channel_tensor * channel_mask.astype(BF)[:, None, :, None]
    mix = jnp.pad(mix.reshape(W * D, W * D), ((0, MIX - W * D), (0, MIX - W * D)))
    own_left = fold_environment(at_start, left_environment[0])
    start, weight = fold_state(my_left, my_right, state_start[0], preconditioner[0])
    right_env = fold_environment(at_end, right_environment[0], came_right)
    handed = []
    sectors = SEC_DEV // 2
    for half in range(2):
        fresh = build_environment(
            half * sectors, sectors, slot, local, own_left, site_previous[0], site_came, mix
        )
        handed.append(passed_along(fresh, "seg", 1))
    mixed = mix_start(mix, right_env, start)

    apply = functools.partial(
        apply_operator,
        entries=entries,
        slots_total=groups * slots,
        tables=(at_start, slot, local),
        left_envs=(own_left, *handed),
    )

    def gather(names, send, own, vectors, weight):
        came = exchange(send.reshape(groups, slots, TILE, FOLD)).reshape(groups * slots, TILE, FOLD)
        result, gram = collect(names, groups, take, my_left, my_right, came, own, vectors, weight)
        return result, exchange(gram)

    send, own = apply("start", fixed_inputs=(mixed,), vectors=())
    product, gram = gather(FIRST, send, own, (start,), weight)
    current, applied, direction, send, own = apply(
        "first", fixed_inputs=(mix, right_env, gram), vectors=(start, product, weight)
    )
    product, gram = gather(LATER, send, own, (applied, direction, current), weight)
    current, applied, direction, send, own = apply(
        "later",
        fixed_inputs=(mix, right_env, gram),
        vectors=(current, applied, direction, product, weight),
    )
    product, gram = gather(LAST, send, own, (applied, direction, current), None)
    state, energy = finish(entries, gram, current, direction)
    return (state[None], energy)


def solution(mesh):
    in_specs = (
        P("seg", "sec", None, None),
        P("seg", "sec", None, None),
        P("seg", "sec", None, None),
        P("seg", "sec", None, None),
        P("seg", "sec", None, None),
        P(),
        P(),
        P(),
        P(),
        P(),
    )
    out_specs = (P("seg", "sec", None, None), P("seg"))
    return jax.shard_map(on_device, mesh=mesh, in_specs=in_specs, out_specs=out_specs, check_vma=False)
```
